32 devices in a mesh: dp: 16 (over z, y, x), mp: 2 (over core).
Axes of the slice: x: 2, y: 2, z: 4, core: 2. Of those that a mesh axis runs over, the one named last changes fastest.
Arguments:
- inputs: float32 [75648, 384], P('dp'), may hold values from -6 to 6
- w_qkv: bfloat16 [3, 384, 384], P(None, 'dp', 'mp'), may hold values from -2 to 2
- b_qv: bfloat16 [2, 6, 64], P(None, 'mp', 'dp'), may hold values from -3 to 3
- w_out: bfloat16 [384, 384], P('mp', 'dp'), may hold values from -1.25 to 1.25
- b_out: bfloat16 [384], P('dp'), may hold values from -3 to 3
- w_up: bfloat16 [384, 1536], P('dp', 'mp'), may hold values from -0.3125 to 0.3125
- b_up: bfloat16 [12, 128], P('mp', 'dp'), may hold values from -3 to 3
- w_down: bfloat16 [1536, 384], P('mp', 'dp'), may hold values from -0.15625 to 0.15625
- b_down: bfloat16 [384], P('dp'), may hold values from -3 to 3
- norm1_gain: bfloat16 [384], P('dp'), may hold values from 0.099609375 to 1.8984375
- norm1_shift: bfloat16 [384], P('dp'), may hold values from -3 to 3
- norm2_gain: bfloat16 [384], P('dp'), may hold values from 0.099609375 to 1.8984375
- norm2_shift: bfloat16 [384], P('dp'), may hold values from -3 to 3
- grad_out: float32 [75648, 384], P('dp'), may hold values from -6 to 6
Outputs:
- output: float32 [75648, 384], P('dp')
- grad_input: float32 [75648, 384], P('dp')
- grad_w_qkv: float32 [3, 384, 384], P(None, 'dp', 'mp')
- grad_b_qv: float32 [2, 6, 64], P(None, 'mp', 'dp')
- grad_w_out: float32 [384, 384], P('mp', 'dp')
- grad_b_out: float32 [384], P('dp')
- grad_w_up: float32 [384, 1536], P('dp', 'mp')
- grad_b_up: float32 [12, 128], P('mp', 'dp')
- grad_w_down: float32 [1536, 384], P('mp', 'dp')
- grad_b_down: float32 [384], P('dp')
- grad_norm1_gain: float32 [384], P('dp')
- grad_norm1_shift: float32 [384], P('dp')
- grad_norm2_gain: float32 [384], P('dp')
- grad_norm2_shift: float32 [384], P('dp')
The draws below stay inside these ranges and needn't reach their ends.
All inputs are finite; a program needn't handle non-finite values.
Results may differ from the reference program's by a relative error of at most 0.017.
Values may be sent and summed in bfloat16 or wider, within the bound.
No kernel may reach another device: no remote copies, remote signals or barrier semaphores. Data moves between devices by JAX's collectives and lax.ppermute only.
A program may use at most 256 MiB of HBM per device.

```python
import jax
import jax.numpy as jnp
from jax import lax

D = 384
HEADS = 6
HEAD_DIM = 64
FF = 1536
SEQ = 197
TOKENS = 75648


def draw_w_qkv(key, part):
    width = HEADS * HEAD_DIM
    base = jnp.clip(jax.random.normal(key, (3, D, width), jnp.float32), -4.0, 4.0) * D ** (-0.5)
    return base.astype(jnp.bfloat16)


def block_scale(rng, dims, cuts, low, high):
    loudness = 1.0
    for dim, shards_of in cuts:
        draws = jax.random.uniform(jax.random.fold_in(jax.random.fold_in(rng, 6), dim), (shards_of,), jnp.float32, low / len(cuts), high / len(cuts))
        loudness = loudness * jnp.repeat(jnp.exp(draws), dims[dim] // shards_of).reshape((-1,) + (1,) * (len(dims) - 1 - dim))
    return loudness


def noise(stream_key, extent, scale, limit, cuts=(), dtype=jnp.bfloat16):
    array = scale * jax.random.normal(stream_key, extent, jnp.float32)
    if cuts:
        array = array * block_scale(stream_key, extent, cuts, -0.22, 0.18)
    return jnp.clip(array, -limit, limit).astype(dtype)


def setup_inputs(seed: int = 0) -> dict:
    key_of = jax.random.split(jax.random.key(seed), 15)
    return {
        "inputs": noise(key_of[0], (TOKENS, D), 1.0, 6.0, ((0, 16),), jnp.float32),
        "w_qkv": draw_w_qkv(jax.random.fold_in(key_of[14], 71), 0),
        "b_qv": noise(key_of[2], (2, HEADS, HEAD_DIM), 0.5, 3.0, ((1, 2), (2, 16))),
        "w_out": noise(key_of[3], (HEADS * HEAD_DIM, D), (HEADS * HEAD_DIM // 16) ** -0.5, 1.25, ((0, 2), (1, 16))),
        "b_out": noise(key_of[4], (D,), 0.5, 3.0, ((0, 16),)),
        "w_up": noise(key_of[5], (D, FF), D ** -0.5, 0.3125, ((0, 16), (1, 2))),
        "b_up": noise(key_of[6], (FF // 128, 128), 0.5, 3.0, ((0, 2), (1, 16))),
        "w_down": noise(key_of[7], (FF, D), FF ** -0.5, 0.15625, ((0, 2), (1, 16))),
        "b_down": noise(key_of[8], (D,), 0.5, 3.0, ((0, 16),)),
        "norm1_gain": jnp.clip(1.0 + 0.18 * jax.random.normal(key_of[9], (D,), jnp.float32), 0.099609375, 1.8984375).astype(jnp.bfloat16),
        "norm1_shift": noise(key_of[10], (D,), 0.5, 3.0, ((0, 16),)),
        "norm2_gain": jnp.clip(1.0 + 0.18 * jax.random.normal(key_of[11], (D,), jnp.float32), 0.099609375, 1.8984375).astype(jnp.bfloat16),
        "norm2_shift": noise(key_of[12], (D,), 0.5, 3.0, ((0, 16),)),
        "grad_out": noise(key_of[13], (TOKENS, D), 1.0, 6.0, ((0, 16),), jnp.float32),
    }


epsilon = 1e-06
root_half = 0.7071067811865476
inv_root_tau = 0.3989422804014327

def lowered(values):
    return lax.optimization_barrier(values.astype(jnp.bfloat16))

def layer_norm(rows, gain, shift):
    center = rows - lax.optimization_barrier(jnp.mean(rows, axis=-1, keepdims=True))
    inverse = lax.rsqrt(lax.optimization_barrier(jnp.mean(center * center, axis=-1, keepdims=True)) + epsilon)
    normal = center * inverse
    return (normal * gain + shift, normal, inverse)

def norm_back(grad_normed, normal, inverse, gain):
    scaled = grad_normed * gain
    first = lax.optimization_barrier(jnp.mean(scaled, axis=-1, keepdims=True))
    second = lax.optimization_barrier(jnp.mean(scaled * normal, axis=-1, keepdims=True))
    grad_rows = inverse * (scaled - first - normal * second)
    return (grad_rows, lax.optimization_barrier(jnp.sum(grad_normed * normal, axis=0)), lax.optimization_barrier(jnp.sum(grad_normed, axis=0)))

def gelu_value(pre):
    return 0.5 * pre * (1.0 + jax.scipy.special.erf(pre * root_half))

def gelu_slope(pre):
    return 0.5 * (1.0 + jax.scipy.special.erf(pre * root_half)) + pre * jnp.exp(-0.5 * pre * pre) * inv_root_tau

def block_pass(inputs, grad_out, params):
    f32 = jnp.float32
    w_qkv, b_qv, w_out, b_out, w_up, b_up, w_down, b_down, gain1, shift1, gain2, shift2 = params
    rows = inputs.shape[0]
    images = rows // SEQ
    width = w_qkv.shape[2]
    heads = width // HEAD_DIM
    scale = HEAD_DIM ** (-0.5)
    normed1_full, hat1, inv1 = layer_norm(inputs, gain1, shift1)
    normed1 = lowered(normed1_full)
    bias3 = jnp.stack([b_qv[0], jnp.zeros_like(b_qv[0]), b_qv[1]])[:, None, :]
    qkv = lowered(jnp.einsum('rd,tdc->trc', normed1.astype(f32), w_qkv.astype(f32)) + bias3)
    shaped = qkv.astype(f32).reshape(3, images, SEQ, heads, HEAD_DIM)
    scores = jnp.einsum('bqhd,bkhd->bhqk', shaped[0], shaped[1]) * scale
    top = lax.optimization_barrier(jnp.max(scores, axis=-1, keepdims=True))
    log_total = jnp.log(lax.optimization_barrier(jnp.sum(jnp.exp(scores - top), axis=-1, keepdims=True))) + top
    probs = lowered(jnp.exp(scores - log_total))
    mixed = lowered(jnp.einsum('bhqk,bkhd->bqhd', probs.astype(f32), shaped[2])).reshape(rows, width)
    resid = inputs + jnp.dot(mixed, w_out, preferred_element_type=f32) + b_out
    normed2_full, hat2, inv2 = layer_norm(resid, gain2, shift2)
    normed2 = lowered(normed2_full)
    hidden_pre = jnp.dot(normed2, w_up, preferred_element_type=f32) + b_up
    hidden = lowered(gelu_value(hidden_pre))
    output = resid + jnp.dot(hidden, w_down, preferred_element_type=f32) + b_down
    grad_low = lowered(grad_out)
    grad_b_down = lax.optimization_barrier(jnp.sum(grad_out, axis=0))
    grad_w_down = jnp.dot(hidden.T, grad_low, preferred_element_type=f32)
    grad_pre = jnp.dot(grad_low, w_down.T, preferred_element_type=f32) * gelu_slope(hidden_pre)
    grad_pre_low = lowered(grad_pre)
    grad_b_up = lax.optimization_barrier(jnp.sum(grad_pre, axis=0))
    grad_w_up = jnp.dot(normed2.T, grad_pre_low, preferred_element_type=f32)
    grad_normed2 = jnp.dot(grad_pre_low, w_up.T, preferred_element_type=f32)
    grad_back2, grad_gain2, grad_shift2 = norm_back(grad_normed2, hat2, inv2, gain2)
    grad_resid = grad_out + grad_back2
    grad_resid_low = lowered(grad_resid)
    grad_b_out = lax.optimization_barrier(jnp.sum(grad_resid, axis=0))
    grad_w_out = jnp.dot(mixed.T, grad_resid_low, preferred_element_type=f32)
    grad_mixed = lowered(jnp.dot(grad_resid_low, w_out.T, preferred_element_type=f32))
    grad_shaped = grad_mixed.astype(f32).reshape(images, SEQ, heads, HEAD_DIM)
    exact = jnp.exp(scores - log_total)
    grad_values = jnp.einsum('bhqk,bqhd->bkhd', probs.astype(f32), grad_shaped)
    grad_probs = jnp.einsum('bqhd,bkhd->bhqk', grad_shaped, shaped[2])
    delta = lax.optimization_barrier(jnp.sum(exact * grad_probs, axis=-1, keepdims=True))
    grad_scores = lowered(exact * (grad_probs - delta) * scale).astype(f32)
    grad_queries = jnp.einsum('bhqk,bkhd->bqhd', grad_scores, shaped[1])
    grad_keys = jnp.einsum('bhqk,bqhd->bkhd', grad_scores, shaped[0])
    grad_three = jnp.stack([grad_queries, grad_keys, grad_values]).reshape(3, rows, width)
    grad_b_qv = jnp.stack([lax.optimization_barrier(jnp.sum(grad_three[0], axis=0)), lax.optimization_barrier(jnp.sum(grad_three[2], axis=0))])
    grad_qkv = lowered(grad_three)
    grad_w_qkv = jnp.einsum('rd,trc->tdc', normed1.astype(f32), grad_qkv.astype(f32))
    grad_normed1 = jnp.einsum('trc,tdc->rd', grad_qkv.astype(f32), w_qkv.astype(f32))
    grad_back1, grad_gain1, grad_shift1 = norm_back(grad_normed1, hat1, inv1, gain1)
    grad_input = grad_resid + grad_back1
    grads = (grad_w_qkv, grad_b_qv, grad_w_out, grad_b_out, grad_w_up, grad_b_up, grad_w_down, grad_b_down, grad_gain1, grad_shift1, grad_gain2, grad_shift2)
    return (output, grad_input, grads)

def reference(inputs, w_qkv, b_qv, w_out, b_out, w_up, b_up, w_down, b_down, norm1_gain, norm1_shift, norm2_gain, norm2_shift, grad_out):
    f32 = jnp.float32
    width = HEADS * HEAD_DIM
    params = (w_qkv, b_qv.astype(f32).reshape(2, width), w_out, b_out.astype(f32), w_up, b_up.astype(f32).reshape(FF), w_down, b_down.astype(f32), norm1_gain.astype(f32), norm1_shift.astype(f32), norm2_gain.astype(f32), norm2_shift.astype(f32))
    group = 16 * SEQ
    blocks = inputs.shape[0] // group
    input_blocks = inputs.reshape(blocks, group, D)
    grad_blocks = grad_out.reshape(blocks, group, D)
    zeros = (jnp.zeros((3, D, width), f32), jnp.zeros((2, width), f32), jnp.zeros((width, D), f32), jnp.zeros((D,), f32), jnp.zeros((D, FF), f32), jnp.zeros((FF,), f32), jnp.zeros((FF, D), f32), jnp.zeros((D,), f32), jnp.zeros((D,), f32), jnp.zeros((D,), f32), jnp.zeros((D,), f32), jnp.zeros((D,), f32))

    def advance(carry, pair):
        output, grad_input, grads = block_pass(pair[0], pair[1], params)
        return (jax.tree.map(lambda left, right: left + right, carry, grads), (output, grad_input))
    totals, (outputs, grad_inputs) = lax.scan(advance, zeros, (input_blocks, grad_blocks))
    return (outputs.reshape(-1, D), grad_inputs.reshape(-1, D), totals[0], totals[1].reshape(2, HEADS, HEAD_DIM), totals[2], totals[3], totals[4], totals[5].reshape(FF // 128, 128), totals[6], totals[7], totals[8], totals[9], totals[10], totals[11])
```

```python
import jax
import jax.numpy as jnp
from jax import lax
from jax.sharding import PartitionSpec as P

HEAD_DIM = 64
SEQ = 197
PAD = 208

EPS = 1e-06
ROOT_HALF = 0.7071067811865476
INV_ROOT_TAU = 0.3989422804014327


f32 = jnp.float32
bf16 = jnp.bfloat16


def nt(a, b):
    return lax.dot_general(a, b, (((1,), (1,)), ((), ())), preferred_element_type=f32)


def tn(a, b):
    return lax.dot_general(a, b, (((0,), (0,)), ((), ())), preferred_element_type=f32)


def nn(a, b):
    return lax.dot_general(a, b, (((1,), (0,)), ((), ())), preferred_element_type=f32)


def digits(count):
    bits = count.bit_length() - 1
    out = []
    while bits > 0:
        width = 2 if bits % 2 == 0 else 1
        bits -= width
        out.append((bits, width))
    return out


def swap(x, axis, count, mask):
    return lax.ppermute(x, axis, [(i, i ^ mask) for i in range(count)])


def ordered(blocks, digit, axis):
    count = len(blocks)
    bit = 1
    while bit < count:
        flip = (digit & bit) != 0
        blocks = [jnp.where(flip, blocks[p ^ bit], blocks[p]) for p in range(count)]
        bit *= 2
    return jnp.stack(blocks, axis)


def gather_rows(x, count):
    me = lax.axis_index("dp")
    cur = x[None]
    for shift, width in digits(count):
        blocks = [cur] + [swap(cur, "dp", count, d << shift) for d in range(1, 1 << width)]
        cur = ordered(blocks, (me >> shift) & ((1 << width) - 1), 1)
        cur = cur.reshape((-1,) + x.shape)
    return cur.reshape(-1, x.shape[1])


def scatter_rows(g, count):
    me = lax.axis_index("dp")
    rows = g.shape[0] // count
    cur = g.reshape(count, rows, g.shape[1])
    for shift, width in reversed(digits(count)):
        radix = 1 << width
        cur = cur.reshape((-1, radix) + cur.shape[1:])
        digit = (me >> shift) & (radix - 1)
        total = lax.dynamic_index_in_dim(cur, digit, 1, False).astype(f32)
        for d in range(1, radix):
            part = lax.dynamic_index_in_dim(cur, digit ^ d, 1, False)
            total = total + swap(part, "dp", count, d << shift).astype(f32)
        cur = total.astype(bf16) if shift + width < count.bit_length() - 1 else total
    return cur.reshape(rows, g.shape[1])


def mine_first(pair, core):
    return jnp.where(core == 0, pair, pair[::-1])


def normalise(x):
    center = x - jnp.mean(x, axis=-1, keepdims=True)
    inverse = lax.rsqrt(jnp.mean(center * center, axis=-1, keepdims=True) + EPS)
    return center * inverse, inverse


def norm_back(grad, hat, inverse, gain):
    scaled = grad * gain
    first = jnp.mean(scaled, axis=-1, keepdims=True)
    second = jnp.mean(scaled * hat, axis=-1, keepdims=True)
    return inverse * (scaled - first - hat * second)


def head_columns(h):
    m, k = divmod(h, 3)
    base = m * 9 * HEAD_DIM + k * HEAD_DIM
    return [slice(base + t * 3 * HEAD_DIM, base + t * 3 * HEAD_DIM + HEAD_DIM) for t in range(3)]


def attend(x, wq, bias, gain, shift):
    images = x.shape[0]
    hat, _ = normalise(x)
    normed = (hat * gain + shift).astype(bf16)
    qkv = (jnp.einsum("brd,dc->brc", normed, wq, preferred_element_type=f32) + bias).astype(bf16)
    pts, mixed = [], []
    for h in range(6):
        cq, ck, cv = head_columns(h)
        st = jnp.einsum("bkd,bqd->bkq", qkv[:, :, ck], qkv[:, :, cq], preferred_element_type=f32)
        st = st * HEAD_DIM**-0.5
        row = lax.broadcasted_iota(jnp.int32, st.shape, 1)
        st = jnp.where(row < SEQ, st, -1e30)
        e = jnp.exp(st - jnp.max(st, axis=1, keepdims=True))
        pt = (e / jnp.sum(e, axis=1, keepdims=True)).astype(bf16)
        pts.append(pt)
        mixed.append(
            jnp.einsum("bkd,bkq->bdq", qkv[:, :, cv], pt, preferred_element_type=f32).astype(bf16)
        )
    return qkv, jnp.stack(pts, 1), jnp.concatenate(mixed, 1)


def feed(x, gout, mixed_t, wot, bo, gain, shift, wu, bu, wdt, bd):
    images = x.shape[0]
    rows = images * PAD
    mixed = mixed_t.transpose(0, 2, 1).reshape(rows, -1)
    x = x.reshape(rows, -1)
    gout = gout.reshape(rows, -1)
    resid = x + nt(mixed, wot) + bo
    hat, inverse = normalise(resid)
    normed = (hat * gain + shift).astype(bf16)
    pre = nn(normed, wu) + bu
    phi = 0.5 * (1.0 + lax.erf(pre * ROOT_HALF))
    hidden = (pre * phi).astype(bf16)
    slope = phi + pre * jnp.exp(-0.5 * pre * pre) * INV_ROOT_TAU
    output = resid + nt(hidden, wdt) + bd
    glow = gout.astype(bf16)
    gpre = nn(glow, wdt) * slope
    gprel = gpre.astype(bf16)
    dwdt = tn(glow, hidden)
    dwu = tn(normed, gprel)
    gn = nt(gprel, wu)
    gres = gout + norm_back(gn, hat, inverse, gain)
    gresl = gres.astype(bf16)
    dwot = tn(gresl, mixed)
    gmixed = nn(gresl, wot).astype(bf16)
    vecs = jnp.stack([gres.sum(0), gout.sum(0), (gn * hat).sum(0), gn.sum(0)])
    shape = (images, PAD, -1)
    return (
        output.astype(bf16).reshape(shape),
        gres.reshape(shape),
        gmixed.reshape(shape),
        dwot,
        dwu,
        dwdt,
        vecs,
        gpre.sum(0)[None],
    )


def attend_back(x, gres, gmixed, qkv, pts, wq, gain, shift):
    images = x.shape[0]
    rows = images * PAD
    scale = HEAD_DIM**-0.5
    parts = [None] * 18
    for h in range(6):
        cq, ck, cv = head_columns(h)
        q, k, v = qkv[:, :, cq], qkv[:, :, ck], qkv[:, :, cv]
        do = gmixed[:, :, h * HEAD_DIM : (h + 1) * HEAD_DIM]
        pt = pts[:, h]
        dv = jnp.einsum("bkq,bqd->bkd", pt, do, preferred_element_type=f32)
        dp = jnp.einsum("bkd,bqd->bkq", v, do, preferred_element_type=f32)
        p = pt.astype(f32)
        delta = jnp.sum(p * dp, axis=1, keepdims=True)
        ds = (p * (dp - delta) * scale).astype(bf16)
        dk = jnp.einsum("bkq,bqd->bkd", ds, q, preferred_element_type=f32)
        dq = jnp.einsum("bkq,bkd->bqd", ds, k, preferred_element_type=f32)
        m, j = divmod(h, 3)
        parts[m * 9 + j], parts[m * 9 + 3 + j], parts[m * 9 + 6 + j] = dq, dk, dv
    dqkv = jnp.concatenate(parts, -1).reshape(rows, -1)
    x = x.reshape(rows, -1)
    hat, inverse = normalise(x)
    normed = (hat * gain + shift).astype(bf16)
    low = dqkv.astype(bf16)
    dwq = tn(normed, low)
    gn = nt(low, wq)
    gin = gres.reshape(rows, -1) + norm_back(gn, hat, inverse, gain)
    vecs = jnp.stack([(gn * hat).sum(0), gn.sum(0)])
    return gin.astype(bf16).reshape(images, PAD, -1), dwq, dqkv.sum(0)[None], vecs


def per_device(dp, *args):
    (inputs, w_qkv, b_qv, w_out, b_out, w_up, b_up, w_down, b_down, g1, s1, g2, s2, grad_out) = args
    core = lax.axis_index("mp")
    rows, depth = inputs.shape
    half = rows // 2
    images = half // SEQ
    share = depth // dp

    def vec(v):
        return v.reshape(share, 1)

    bq = b_qv.transpose(2, 0, 1)
    first = jnp.concatenate([w_qkv.transpose(1, 0, 2).reshape(share, -1)], 1)
    rest = jnp.concatenate([w_out.T, w_up, w_down.T], 1)
    small = jnp.concatenate([b_qv.reshape(-1), b_up.reshape(-1)] + [v for v in (b_out, b_down, g1, s1, g2, s2)])
    small = jnp.pad(small, (0, -small.shape[0] % 128))[None]

    first_all = gather_rows(first, dp)
    small_all = gather_rows(small, dp)
    rest_all = gather_rows(rest, dp)

    def both(x):
        other = swap(x, "mp", 2, 1)
        return jnp.where(core == 0, x, other), jnp.where(core == 0, other, x)

    wq = jnp.concatenate(both(first_all), 1)
    small2 = jnp.stack(both(small_all)).astype(f32)
    rest0, rest1 = both(rest_all)
    c_out = w_out.shape[0]
    c_up = w_up.shape[1]
    cut = [(0, c_out), (c_out, c_out + c_up), (c_out + c_up, c_out + 2 * c_up)]
    wot, wu, wdt = [jnp.concatenate([rest0[:, a:b], rest1[:, a:b]], 1) for a, b in cut]

    nb = b_qv.size
    nu = b_up.size
    bqv = small2[:, :, :nb].reshape((2, dp) + b_qv.shape)
    bqv = bqv.transpose(0, 2, 3, 1, 4).reshape(2, 2, -1)
    bias = jnp.stack([bqv[:, 0], jnp.zeros_like(bqv[:, 0]), bqv[:, 1]], 1).reshape(1, -1)
    bu = small2[:, :, nb : nb + nu].reshape((2, dp) + b_up.shape)
    bu = bu.transpose(0, 2, 1, 3).reshape(1, -1)
    vs = small2[0, :, nb + nu : nb + nu + 6 * share].reshape(dp, 6, share)
    vs = vs.transpose(1, 0, 2).reshape(6, 1, depth)
    bo, bd, gain1, shift1, gain2, shift2 = [vs[i] for i in range(6)]

    def local(a):
        a = lax.dynamic_slice_in_dim(a, core * half, half, 0)
        return jnp.pad(a.reshape(images, SEQ, depth), ((0, 0), (0, PAD - SEQ), (0, 0)))

    x = local(inputs)
    gout = local(grad_out)

    qkv, pts, mixed_t = attend(x, wq, bias, gain1, shift1)
    output, gres, gmixed, dwot, dwu, dwdt, vec2, gbu = feed(
        x, gout, mixed_t, wot, bo, gain2, shift2, wu, bu, wdt, bd
    )

    def whole_rows(a):
        mine = a[:, :SEQ].reshape(half, depth)
        other = swap(mine, "mp", 2, 1)
        return jnp.concatenate(
            [jnp.where(core == 0, mine, other), jnp.where(core == 0, other, mine)], 0
        ).astype(f32)

    def reduce_cores(g):
        g = g.reshape(g.shape[0], 2, -1).astype(bf16)
        own = lax.dynamic_index_in_dim(g, core, 1, False)
        give = lax.dynamic_index_in_dim(g, 1 - core, 1, False)
        return (own.astype(f32) + swap(give, "mp", 2, 1).astype(f32)).astype(bf16)

    grest = scatter_rows(jnp.concatenate([reduce_cores(g) for g in (dwot, dwu, dwdt)], 1), dp)
    out_full = whole_rows(output)

    gin, dwq, dbq, vec1 = attend_back(x, gres, gmixed, qkv, pts, wq, gain1, shift1)
    gfirst = scatter_rows(reduce_cores(dwq), dp)
    gin_full = whole_rows(gin)

    dbq = dbq.reshape(2, 3, 3, HEAD_DIM)[:, ::2]
    smalls = jnp.concatenate([dbq.reshape(-1), gbu.reshape(-1), vec2.reshape(-1), vec1.reshape(-1)])
    n_small = smalls.shape[0]
    smalls = jnp.pad(smalls, (0, -n_small % 1024)).reshape(-1, 128)
    smalls = lax.psum(smalls, ("dp", "mp")).reshape(-1)
    place = lax.axis_index("dp")
    a = dbq.size
    gbqv = lax.dynamic_index_in_dim(smalls[:a].reshape(2, 2, 3, HEAD_DIM), core, 0, False)
    gbqv = lax.dynamic_slice_in_dim(gbqv, place * b_qv.shape[2], b_qv.shape[2], 2)
    b = a + gbu.size
    gbup = lax.dynamic_index_in_dim(smalls[a:b].reshape(2, -1, 128), core, 0, False)
    gbup = lax.dynamic_slice_in_dim(gbup, place * b_up.shape[1], b_up.shape[1], 1)
    vecs = smalls[b : b + 6 * depth].reshape(6, depth)
    vecs = lax.dynamic_slice_in_dim(vecs, place * share, share, 1)
    gbo, gbd, gg2, gs2, gg1, gs1 = [vecs[i] for i in range(6)]

    gw_qkv = gfirst.reshape(share, 3, -1).transpose(1, 0, 2)
    gw_out, gw_up, gw_down = [grest[:, p:q] for p, q in cut]
    return (
        out_full,
        gin_full,
        gw_qkv,
        gbqv,
        gw_out.T,
        gbo,
        gw_up,
        gbup,
        gw_down.T,
        gbd,
        gg1,
        gs1,
        gg2,
        gs2,
    )


def solution(mesh):
    specs = (
        P("dp", None),
        P(None, "dp", "mp"),
        P(None, "mp", "dp"),
        P("mp", "dp"),
        P("dp"),
        P("dp", "mp"),
        P("mp", "dp"),
        P("mp", "dp"),
        P("dp"),
        P("dp"),
        P("dp"),
        P("dp"),
        P("dp"),
    )
    dp = mesh.shape["dp"]

    def run(*args):
        return per_device(dp, *args)

    return jax.shard_map(
        run,
        mesh=mesh,
        in_specs=specs + (P("dp", None),),
        out_specs=(P("dp", None),) + specs,
        check_vma=False,
    )
```

```python
import jax
import jax.numpy as jnp
from jax import lax
from jax.experimental import pallas as pl
from jax.experimental.pallas import tpu as pltpu
from jax.sharding import PartitionSpec as P

HEAD_DIM = 64
SEQ = 197
PAD = 208
EPS = 1e-06
ROOT_HALF = 0.7071067811865476
INV_ROOT_TAU = 0.3989422804014327
D = 384
FF = 1536


f32 = jnp.float32
bf16 = jnp.bfloat16


def nt(a, b):
    return lax.dot_general(a, b, (((1,), (1,)), ((), ())), preferred_element_type=f32)


def nn(a, b):
    return lax.dot_general(a, b, (((1,), (0,)), ((), ())), preferred_element_type=f32)


def normalise(x):
    center = x - jnp.mean(x, axis=-1, keepdims=True)
    inverse = lax.rsqrt(jnp.mean(center * center, axis=-1, keepdims=True) + EPS)
    return center * inverse, inverse


def norm_back(grad, hat, inverse, gain):
    scaled = grad * gain
    first = jnp.mean(scaled, axis=-1, keepdims=True)
    second = jnp.mean(scaled * hat, axis=-1, keepdims=True)
    return inverse * (scaled - first - hat * second)


def whole(shape):
    return pl.BlockSpec(shape, lambda i: (0,) * len(shape))


def image(shape):
    return pl.BlockSpec(shape, lambda i: (i,) + (0,) * (len(shape) - 1))


LIMIT = 60 * 1024 * 1024


def attend_kernel(x_ref, wq_ref, bq_ref, vec_ref, qkv_ref, pt_ref, mt_ref):
    hat, _ = normalise(x_ref[0])
    normed = (hat * vec_ref[0:1] + vec_ref[1:2]).astype(bf16)
    for c in range(0, 3 * D, 384):
        qkv_ref[0, :, c : c + 384] = (
            nn(normed, wq_ref[:, c : c + 384]) + bq_ref[:, c : c + 384]
        ).astype(bf16)
    lane = lax.broadcasted_iota(jnp.int32, (PAD, 128), 1)
    tail = lax.broadcasted_iota(jnp.int32, (16, PAD), 0) < SEQ - (PAD - 16)
    for j in range(3):
        cols = slice(j * 128, j * 128 + 128)
        q = qkv_ref[0, :, j * 128 : j * 128 + 128] * jnp.asarray(0.125, bf16)
        k = qkv_ref[0, :, D + j * 128 : D + j * 128 + 128]
        v = qkv_ref[0, :, 2 * D + j * 128 : 2 * D + j * 128 + 128]
        vt = v.T
        for e in range(2):
            kh = jnp.where((lane < 64) == (e == 0), k, jnp.zeros_like(k))
            st = nt(kh, q)
            body, end = st[: PAD - 16], jnp.where(tail, st[PAD - 16 :], -1e30)
            top = jnp.maximum(
                jnp.max(body, axis=0, keepdims=True), jnp.max(end, axis=0, keepdims=True)
            )
            st = jnp.concatenate([body, end], 0)
            ex = jnp.exp(st - top)
            total = jnp.sum(ex, axis=0, keepdims=True)
            pt = (ex * (1.0 / total)).astype(bf16)
            pt_ref[0, 2 * j + e] = pt
            mt_ref[0, j * 128 + e * 64 : j * 128 + e * 64 + 64] = nn(
                vt[e * 64 : e * 64 + 64], pt
            ).astype(bf16)


def attend(x, wq, bq, vec):
    n = x.shape[0]
    return pl.pallas_call(
        attend_kernel,
        grid=(n,),
        in_specs=[image((1, PAD, D)), whole((D, 3 * D)), whole((1, 3 * D)), whole((8, D))],
        out_specs=[image((1, PAD, 3 * D)), image((1, 6, PAD, PAD)), image((1, D, PAD))],
        out_shape=[
            jax.ShapeDtypeStruct((n, PAD, 3 * D), bf16),
            jax.ShapeDtypeStruct((n, 6, PAD, PAD), bf16),
            jax.ShapeDtypeStruct((n, D, PAD), bf16),
        ],
        compiler_params=pltpu.CompilerParams(vmem_limit_bytes=LIMIT),
        cost_estimate=pl.CostEstimate(flops=4 * 10**9, bytes_accessed=2 * 10**7, transcendentals=0),
        name="attend",
    )(x, wq, bq, vec)


def feed_kernel(
    x_ref, g_ref, mt_ref, wot_ref, wu_ref, wdt_ref, vec_ref, bu_ref,
    out_ref, gres_ref, gm_ref, dw_ref, gvec_ref, gbu_ref,
    hid_ref, gpl_ref, aco_ref, acu_ref, acd_ref, hat_ref, res_ref,
):
    step = pl.program_id(0)
    last = pl.num_programs(0) - 1
    group = x_ref.shape[0]
    rows = group * PAD

    @pl.when(step == 0)
    def _():
        aco_ref[...] = jnp.zeros_like(aco_ref)
        acu_ref[...] = jnp.zeros_like(acu_ref)
        acd_ref[...] = jnp.zeros_like(acd_ref)
        gvec_ref[...] = jnp.zeros_like(gvec_ref)
        gbu_ref[...] = jnp.zeros_like(gbu_ref)

    bo, gain, shift, bd = [vec_ref[i : i + 1] for i in range(4)]
    x = x_ref[...].reshape(rows, D)
    mixed = jnp.concatenate([mt_ref[i].T for i in range(group)], 0)
    resid = x + nt(mixed, wot_ref[...]) + bo
    res_ref[...] = resid
    hat, inverse = normalise(resid)
    hat_ref[...] = hat
    normed = (hat * gain + shift).astype(bf16)
    glow = g_ref[...].reshape(rows, D).astype(bf16)
    normed_t = normed.T
    glow_t = glow.T
    width = 256
    for c in range(0, FF, width):
        cols = slice(c, c + width)
        pre = nn(normed, wu_ref[:, cols]) + bu_ref[:, cols]
        phi = 0.5 + 0.5 * lax.erf(pre * ROOT_HALF)
        slope = phi + pre * (jnp.exp(-0.5 * pre * pre) * INV_ROOT_TAU)
        hid = (pre * phi).astype(bf16)
        hid_ref[:, cols] = hid
        gpre = nn(glow, wdt_ref[:, cols]) * slope
        gbu_ref[:, cols] += jnp.sum(gpre, axis=0, keepdims=True)
        gpl = gpre.astype(bf16)
        gpl_ref[:, cols] = gpl
        acd_ref[:, cols] += nn(glow_t, hid)
        acu_ref[:, cols] += nn(normed_t, gpl)
    out = res_ref[...] + nt(hid_ref[...], wdt_ref[...]) + bd
    out_ref[...] = out.astype(bf16).reshape(group, PAD, D)
    gn = nt(gpl_ref[...], wu_ref[...])
    hat = hat_ref[...]
    gout = g_ref[...].reshape(rows, D)
    gres = gout + norm_back(gn, hat, inverse, gain)
    gres_ref[...] = gres.reshape(group, PAD, D)
    gresl = gres.astype(bf16)
    gvec_ref[0:1] += jnp.sum(gres, axis=0, keepdims=True)
    gvec_ref[1:2] += jnp.sum(gout, axis=0, keepdims=True)
    gvec_ref[2:3] += jnp.sum(gn * hat, axis=0, keepdims=True)
    gvec_ref[3:4] += jnp.sum(gn, axis=0, keepdims=True)
    gm_ref[...] = nn(gresl, wot_ref[...]).astype(bf16).reshape(group, PAD, D)
    for i in range(group):
        aco_ref[...] += nn(mt_ref[i], gresl[i * PAD : (i + 1) * PAD])

    @pl.when(step == last)
    def _():
        out_t = aco_ref[...].T.astype(bf16)
        for m in range(2):
            dw_ref[m, :, : FF // 2] = acu_ref[:, m * FF // 2 : (m + 1) * FF // 2].astype(bf16)
            dw_ref[m, :, FF // 2 : FF] = acd_ref[:, m * FF // 2 : (m + 1) * FF // 2].astype(bf16)
            dw_ref[m, :, FF:] = out_t[:, m * D // 2 : (m + 1) * D // 2]


def feed(x, gout, mt, wot, wu, wdt, vec, bu, group=2):
    n = x.shape[0]
    rows = group * PAD
    return pl.pallas_call(
        feed_kernel,
        grid=(n // group,),
        in_specs=[
            image((group, PAD, D)), image((group, PAD, D)), image((group, D, PAD)),
            whole((D, D)), whole((D, FF)), whole((D, FF)), whole((8, D)), whole((1, FF)),
        ],
        out_specs=[
            image((group, PAD, D)), image((group, PAD, D)), image((group, PAD, D)),
            whole((2, D, FF + D // 2)), whole((8, D)), whole((1, FF)),
        ],
        out_shape=[
            jax.ShapeDtypeStruct((n, PAD, D), bf16),
            jax.ShapeDtypeStruct((n, PAD, D), f32),
            jax.ShapeDtypeStruct((n, PAD, D), bf16),
            jax.ShapeDtypeStruct((2, D, FF + D // 2), bf16),
            jax.ShapeDtypeStruct((8, D), f32),
            jax.ShapeDtypeStruct((1, FF), f32),
        ],
        scratch_shapes=[
            pltpu.VMEM((rows, FF), bf16), pltpu.VMEM((rows, FF), bf16),
            pltpu.VMEM((D, D), f32), pltpu.VMEM((D, FF), f32), pltpu.VMEM((D, FF), f32),
            pltpu.VMEM((rows, D), f32), pltpu.VMEM((rows, D), f32),
        ],
        compiler_params=pltpu.CompilerParams(vmem_limit_bytes=LIMIT),
        cost_estimate=pl.CostEstimate(flops=20 * 10**9, bytes_accessed=3 * 10**7, transcendentals=0),
        name="feed",
    )(x, gout, mt, wot, wu, wdt, vec, bu)


def attend_back_kernel(
    x_ref, gres_ref, gm_ref, qkv_ref, pt_ref, wq_ref, vec_ref,
    gin_ref, dwq_ref, dbq_ref, gvec_ref, acq_ref, dq_ref, dqt_ref,
):
    step = pl.program_id(0)
    last = pl.num_programs(0) - 1

    @pl.when(step == 0)
    def _():
        acq_ref[...] = jnp.zeros_like(acq_ref)
        gvec_ref[...] = jnp.zeros_like(gvec_ref)
        dbq_ref[...] = jnp.zeros_like(dbq_ref)

    eighth = jnp.asarray(0.125, bf16)
    lane = lax.broadcasted_iota(jnp.int32, (PAD, 128), 1)
    for j in range(3):
        q = qkv_ref[0, :, j * 128 : j * 128 + 128] * eighth
        kt = (qkv_ref[0, :, D + j * 128 : D + j * 128 + 128] * eighth).T
        v = qkv_ref[0, :, 2 * D + j * 128 : 2 * D + j * 128 + 128]
        do = gm_ref[0, :, j * 128 : j * 128 + 128]
        dk = dv = None
        for e in range(2):
            here = (lane < 64) == (e == 0)
            doh = jnp.where(here, do, jnp.zeros_like(do))
            qh = jnp.where(here, q, jnp.zeros_like(q))
            pt = pt_ref[0, 2 * j + e]
            dvh = nn(pt, doh)
            dp = nt(v, doh)
            p = pt.astype(f32)
            delta = jnp.sum(p * dp, axis=0, keepdims=True)
            ds = (p * (dp - delta)).astype(bf16)
            dkh = nn(ds, qh)
            dqt_ref[j * 128 + e * 64 : j * 128 + e * 64 + 64] = nn(kt[e * 64 : e * 64 + 64], ds)
            dk = dkh if e == 0 else dk + dkh
            dv = dvh if e == 0 else dv + dvh
        dq_ref[:, D + j * 128 : D + j * 128 + 128] = dk.astype(bf16)
        dq_ref[:, 2 * D + j * 128 : 2 * D + j * 128 + 128] = dv.astype(bf16)
        dbq_ref[1:2, j * 128 : j * 128 + 128] += jnp.sum(dv, axis=0, keepdims=True)
    dq = dqt_ref[...].T
    dbq_ref[0:1] += jnp.sum(dq, axis=0, keepdims=True)
    dq_ref[:, :D] = dq.astype(bf16)
    gain, shift = vec_ref[0:1], vec_ref[1:2]
    hat, inverse = normalise(x_ref[0])
    normed_t = (hat * gain + shift).astype(bf16).T
    acq_ref[...] += nn(normed_t, dq_ref[...])
    gn = nt(dq_ref[...], wq_ref[...])
    gvec_ref[0:1] += jnp.sum(gn * hat, axis=0, keepdims=True)
    gvec_ref[1:2] += jnp.sum(gn, axis=0, keepdims=True)
    gin_ref[0] = (gres_ref[0] + norm_back(gn, hat, inverse, gain)).astype(bf16)

    @pl.when(step == last)
    def _():
        for m in range(2):
            for t in range(3):
                a, b = t * D + m * D // 2, t * D + (m + 1) * D // 2
                dwq_ref[m, :, t * D // 2 : (t + 1) * D // 2] = acq_ref[:, a:b].astype(bf16)


def attend_back(x, gres, gm, qkv, pt, wq, vec):
    n = x.shape[0]
    return pl.pallas_call(
        attend_back_kernel,
        grid=(n,),
        in_specs=[
            image((1, PAD, D)), image((1, PAD, D)), image((1, PAD, D)),
            image((1, PAD, 3 * D)), image((1, 6, PAD, PAD)), whole((D, 3 * D)), whole((8, D)),
        ],
        out_specs=[image((1, PAD, D)), whole((2, D, 3 * D // 2)), whole((8, D)), whole((8, D))],
        out_shape=[
            jax.ShapeDtypeStruct((n, PAD, D), bf16),
            jax.ShapeDtypeStruct((2, D, 3 * D // 2), bf16),
            jax.ShapeDtypeStruct((8, D), f32),
            jax.ShapeDtypeStruct((8, D), f32),
        ],
        scratch_shapes=[
            pltpu.VMEM((D, 3 * D), f32), pltpu.VMEM((PAD, 3 * D), bf16), pltpu.VMEM((D, PAD), f32),
        ],
        compiler_params=pltpu.CompilerParams(vmem_limit_bytes=LIMIT),
        cost_estimate=pl.CostEstimate(flops=8 * 10**9, bytes_accessed=3 * 10**7, transcendentals=0),
        name="attend_back",
    )(x, gres, gm, qkv, pt, wq, vec)


def digits(count):
    bits = count.bit_length() - 1
    out = []
    while bits > 0:
        width = 2 if bits % 2 == 0 else 1
        bits -= width
        out.append((bits, width))
    return out


def swap(x, axis, count, mask):
    return lax.ppermute(x, axis, [(i, i ^ mask) for i in range(count)])


def ordered(blocks, digit, axis):
    count = len(blocks)
    bit = 1
    while bit < count:
        flip = (digit & bit) != 0
        blocks = [jnp.where(flip, blocks[p ^ bit], blocks[p]) for p in range(count)]
        bit *= 2
    return jnp.stack(blocks, axis)


def gather_rows(x, count):
    me = lax.axis_index("dp")
    cur = x[None]
    for shift, width in digits(count):
        blocks = [cur] + [swap(cur, "dp", count, d << shift) for d in range(1, 1 << width)]
        cur = ordered(blocks, (me >> shift) & ((1 << width) - 1), 1)
        cur = cur.reshape((-1,) + x.shape)
    return cur


def scatter_rows(cur, count):
    me = lax.axis_index("dp")
    for shift, width in reversed(digits(count)):
        radix = 1 << width
        cur = cur.reshape((-1, radix) + cur.shape[-2:])
        digit = (me >> shift) & (radix - 1)
        total = lax.dynamic_index_in_dim(cur, digit, 1, False).astype(f32)
        for d in range(1, radix):
            part = lax.dynamic_index_in_dim(cur, digit ^ d, 1, False)
            total = total + swap(part, "dp", count, d << shift).astype(f32)
        cur = total.astype(bf16) if shift + width < count.bit_length() - 1 else total
    return cur[0]


def per_device(dp, *args):
    (inputs, w_qkv, b_qv, w_out, b_out, w_up, b_up, w_down, b_down, g1, s1, g2, s2, grad_out) = args
    core = lax.axis_index("mp")
    place = lax.axis_index("dp")
    rows = inputs.shape[0]
    half = rows // 2
    images = half // SEQ
    share = D // dp

    small = [b_qv.reshape(-1), b_up.reshape(-1), b_out, b_down, g1, s1, g2, s2]
    small = jnp.concatenate(small)
    n_small = small.shape[0]
    wide = -(-n_small // share)
    small = jnp.pad(small, (0, wide * share - n_small)).reshape(share, wide)
    small = jnp.pad(small, ((0, 0), (0, 128 - wide)))
    first = jnp.concatenate([w_qkv.transpose(1, 0, 2).reshape(share, -1), small], 1)
    rest = jnp.concatenate([w_up, w_down.T, w_out.T], 1)
    first = gather_rows(first, dp).reshape(D, -1)
    first = [first, swap(first, "mp", 2, 1)]
    rest = gather_rows(rest, dp).reshape(D, -1)
    rest = [rest, swap(rest, "mp", 2, 1)]

    def both(pair, a, b):
        return ordered([x[:, a:b] for x in pair], core, 1)

    n_q = w_qkv.shape[2]
    wq = both(first, 0, 3 * n_q).reshape(D, 2, 3, n_q).transpose(0, 2, 1, 3).reshape(D, 3 * D)
    n_u = w_up.shape[1]
    n_o = w_out.shape[0]
    wu = both(rest, 0, n_u).reshape(D, FF)
    wdt = both(rest, n_u, 2 * n_u).reshape(D, FF)
    wot = both(rest, 2 * n_u, 2 * n_u + n_o).reshape(D, D)

    s = both(first, 3 * n_q, 3 * n_q + wide).astype(f32)
    s = s.reshape(dp, share, 2, wide).transpose(2, 0, 1, 3).reshape(2, dp, -1)
    nb, nu = b_qv.size, b_up.size
    bqv = s[:, :, :nb].reshape(2, dp, 2, 3, -1).transpose(2, 0, 3, 1, 4).reshape(2, D)
    bias = jnp.concatenate([bqv[0], jnp.zeros((D,), f32), bqv[1]])[None]
    bu = s[:, :, nb : nb + nu].reshape((2, dp) + b_up.shape).transpose(0, 2, 1, 3).reshape(1, FF)
    vs = s[0, :, nb + nu : n_small].reshape(dp, 6, share).transpose(1, 0, 2).reshape(6, D)
    vec1 = jnp.concatenate([vs[2:4], jnp.zeros((6, D), f32)])
    vec2 = jnp.concatenate([vs[0:1], vs[4:6], vs[1:2], jnp.zeros((4, D), f32)])

    def local(a):
        a = lax.dynamic_slice_in_dim(a, core * half, half, 0)
        return jnp.pad(a.reshape(images, SEQ, D), ((0, 0), (0, PAD - SEQ), (0, 0)))

    x = local(inputs)
    gout = local(grad_out)

    qkv, pts, mixed_t = attend(x, wq, bias, vec1)
    output, gres, gmixed, grest, gvec2, gbu = feed(x, gout, mixed_t, wot, wu, wdt, vec2, bu)

    def whole_rows(a):
        mine = a[:, :SEQ].reshape(half, D)
        other = swap(mine, "mp", 2, 1)
        return jnp.concatenate(
            [jnp.where(core == 0, mine, other), jnp.where(core == 0, other, mine)], 0
        ).astype(f32)

    def reduce_cores(g):
        own = lax.dynamic_index_in_dim(g, core, 0, False)
        give = lax.dynamic_index_in_dim(g, 1 - core, 0, False)
        total = own.astype(f32) + swap(give, "mp", 2, 1).astype(f32)
        return total.astype(bf16).reshape(dp, share, -1)

    grest = scatter_rows(reduce_cores(grest), dp)
    out_full = whole_rows(output)

    gin, gfirst, dbq, gvec1 = attend_back(x, gres, gmixed, qkv, pts, wq, vec1)

    flat = [dbq[:2], gbu.reshape(-1, D), gvec2[:4], gvec1[:2]]
    flat = jnp.concatenate(flat)
    flat = flat + swap(flat, "mp", 2, 1)
    own = lax.dynamic_index_in_dim(flat[:2].reshape(2, 2, 3, HEAD_DIM), core, 1, False)
    own = own.reshape(2, 3, dp, -1).transpose(2, 0, 1, 3).reshape(dp, nb)
    up = lax.dynamic_index_in_dim(flat[2:6].reshape(2, -1, 128), core, 0, False)
    up = up.reshape(up.shape[0], dp, -1).transpose(1, 0, 2).reshape(dp, nu)
    vec = flat[6:12].reshape(6, dp, share).transpose(1, 0, 2).reshape(dp, 6 * share)
    tail = jnp.concatenate([own, up, vec], 1).astype(bf16)
    width = gfirst.shape[2]
    tail = jnp.pad(tail, ((0, 0), (0, width - n_small)))[:, None]
    gfirst = scatter_rows(jnp.concatenate([reduce_cores(gfirst), tail], 1), dp)
    gin_full = whole_rows(gin)

    tail = gfirst[share]
    gbqv = tail[:nb].reshape(b_qv.shape)
    gbup = tail[nb : nb + nu].reshape(b_up.shape)
    gbo, gbd, gg2, gs2, gg1, gs1 = tail[nb + nu : n_small].reshape(6, share)
    gw_qkv = gfirst[:share].reshape(share, 3, -1).transpose(1, 0, 2)
    return (
        out_full,
        gin_full,
        gw_qkv,
        gbqv,
        grest[:, 2 * n_u :].T,
        gbo,
        grest[:, :n_u],
        gbup,
        grest[:, n_u : 2 * n_u].T,
        gbd,
        gg1,
        gs1,
        gg2,
        gs2,
    )


def solution(mesh):
    specs = (
        P("dp", None),
        P(None, "dp", "mp"),
        P(None, "mp", "dp"),
        P("mp", "dp"),
        P("dp"),
        P("dp", "mp"),
        P("mp", "dp"),
        P("mp", "dp"),
        P("dp"),
        P("dp"),
        P("dp"),
        P("dp"),
        P("dp"),
    )
    dp = mesh.shape["dp"]

    def run(*args):
        return per_device(dp, *args)

    return jax.shard_map(
        run,
        mesh=mesh,
        in_specs=specs + (P("dp", None),),
        out_specs=(P("dp", None),) + specs,
        check_vma=False,
    )
```

```python
import jax
import jax.numpy as jnp
import numpy as np
from jax import lax
from jax.experimental import pallas as pl
from jax.experimental.pallas import tpu as pltpu
from jax.sharding import PartitionSpec as P

HEAD_DIM = 64
SEQ = 197
PAD = 208
EPS = 1e-06
ROOT_HALF = 0.7071067811865476
INV_ROOT_TAU = 0.3989422804014327
D = 384
FF = 1536


f32 = jnp.float32
bf16 = jnp.bfloat16


def nt(a, b):
    return lax.dot_general(a, b, (((1,), (1,)), ((), ())), preferred_element_type=f32)


def nn(a, b):
    return lax.dot_general(a, b, (((1,), (0,)), ((), ())), preferred_element_type=f32)


def normalise(x):
    center = x - jnp.mean(x, axis=-1, keepdims=True)
    inverse = lax.rsqrt(jnp.mean(center * center, axis=-1, keepdims=True) + EPS)
    return center * inverse, inverse


def norm_back(grad, hat, inverse, gain):
    scaled = grad * gain
    first = jnp.mean(scaled, axis=-1, keepdims=True)
    second = jnp.mean(scaled * hat, axis=-1, keepdims=True)
    return inverse * (scaled - first - hat * second)


LIMIT = 60 * 1024 * 1024
ANY = pl.BlockSpec(memory_space=pl.ANY)


def whole(shape):
    return pl.BlockSpec(shape, lambda i, *_: (0,) * len(shape))


def image(shape, base=0):
    return pl.BlockSpec(shape, lambda i, *_: (i + base,) + (0,) * (len(shape) - 1))


def call(kernel, core, grid, ins, in_specs, outs, out_specs, cost, scratch=(), alias=None, name=None):
    return pl.pallas_call(
        kernel,
        grid_spec=pltpu.PrefetchScalarGridSpec(
            num_scalar_prefetch=1,
            grid=(grid,),
            in_specs=in_specs,
            out_specs=out_specs,
            scratch_shapes=list(scratch),
        ),
        out_shape=outs,
        input_output_aliases=alias or {},
        compiler_params=pltpu.CompilerParams(vmem_limit_bytes=LIMIT),
        cost_estimate=pl.CostEstimate(
            flops=cost * 10**9 // 4, bytes_accessed=cost * 3 * 10**6, transcendentals=0
        ),
        name=name,
    )(core, *ins)


def shape(dims, dtype):
    return jax.ShapeDtypeStruct(dims, dtype)


def prepare_kernel(rows, group, core_ref, *refs):
    out_ref = refs[-1]
    sub = lax.broadcasted_iota(jnp.int32, (PAD // 8, 8, D), 1)
    row = lax.broadcasted_iota(jnp.int32, (PAD, D), 0)
    for k in range(group):
        at = SEQ * (pl.program_id(0) * group + k + core_ref[0] * (rows // (2 * SEQ)))
        off = at - first_row(at, rows)
        x = refs[k][...].reshape(PAD // 8, 8, D)
        x = jnp.where(off >= 8, jnp.concatenate([x[1:], x[:1]], 0), x)
        rest = lax.rem(off, 8)
        x = pltpu.roll(x, lax.rem(8 - rest, 8), 1)
        x = jnp.where(sub < 8 - rest, x, jnp.concatenate([x[1:], x[:1]], 0))
        out_ref[k] = jnp.where(row < SEQ, x.reshape(PAD, D), 0.0)


def first_row(at, rows):
    return jnp.minimum(at // 8, (rows - PAD) // 8) * 8


def prepare(core, a, group=2):
    rows = a.shape[0]
    images = rows // (2 * SEQ)

    def spec(k):
        def at(i, core):
            row = first_row(SEQ * (i * group + k + core[0] * images), rows)
            return pl.multiple_of(row, 8), 0

        return pl.BlockSpec((pl.Element(PAD), pl.Element(D)), at)

    return call(
        lambda *r: prepare_kernel(rows, group, *r),
        core,
        images // group,
        [a] * group,
        [spec(k) for k in range(group)],
        shape((images, PAD, D), f32),
        image((group, PAD, D)),
        4,
        name="prepare",
    )


def join_kernel(images, core_ref, mine_ref, other_ref, out_ref, buf, sem):
    step = pl.program_id(0)
    core = core_ref[0]

    @pl.when(step == 0)
    def _():
        for g in range(2 * images):
            @pl.when(core == g // images)
            def _():
                pltpu.make_async_copy(mine_ref.at[g % images], buf.at[g], sem.at[g]).start()

            @pl.when(core != g // images)
            def _():
                pltpu.make_async_copy(other_ref.at[g % images], buf.at[g], sem.at[g]).start()

    for k in range(8):
        g = 8 * step + k
        pltpu.make_async_copy(mine_ref.at[0], buf.at[g], sem.at[g]).wait()
        out_ref[SEQ * k : SEQ * k + SEQ, :] = buf[g, :SEQ, :].astype(f32)


def join(core, mine, other):
    images = mine.shape[0]
    return call(
        lambda *r: join_kernel(images, *r),
        core,
        2 * images // 8,
        [mine, other],
        [ANY, ANY],
        shape((2 * images * SEQ, D), f32),
        pl.BlockSpec((8 * SEQ, D), lambda i, _: (i, 0)),
        5,
        scratch=[pltpu.VMEM((2 * images, PAD, D), bf16), pltpu.SemaphoreType.DMA((2 * images,))],
        name="join",
    )


def attend_body(x_ref, wq_ref, bq_ref, vec_ref, qkv_ref, pt_ref, mt_ref, ht_ref):
    hat, _ = normalise(x_ref[0])
    ht_ref[0] = hat.astype(bf16).T
    normed = (hat * vec_ref[0:1] + vec_ref[1:2]).astype(bf16)
    for c in range(0, 3 * D, 384):
        qkv_ref[0, :, c : c + 384] = (
            nn(normed, wq_ref[:, c : c + 384]) + bq_ref[:, c : c + 384]
        ).astype(bf16)
    lane = lax.broadcasted_iota(jnp.int32, (PAD, 128), 1)
    tail = lax.broadcasted_iota(jnp.int32, (16, PAD), 0) < SEQ - (PAD - 16)
    for j in range(3):
        q = qkv_ref[0, :, j * 128 : j * 128 + 128] * jnp.asarray(0.125, bf16)
        k = qkv_ref[0, :, D + j * 128 : D + j * 128 + 128]
        v = qkv_ref[0, :, 2 * D + j * 128 : 2 * D + j * 128 + 128]
        vt = v.T
        for e in range(2):
            kh = jnp.where((lane < 64) == (e == 0), k, jnp.zeros_like(k))
            st = nt(kh, q)
            body, end = st[: PAD - 16], jnp.where(tail, st[PAD - 16 :], -1e30)
            top = jnp.maximum(
                jnp.max(body, axis=0, keepdims=True), jnp.max(end, axis=0, keepdims=True)
            )
            st = jnp.concatenate([body, end], 0)
            ex = jnp.exp(st - top)
            total = jnp.sum(ex, axis=0, keepdims=True)
            pt = (ex * (1.0 / total)).astype(bf16)
            pt_ref[0, 2 * j + e] = pt
            mt_ref[0, j * 128 + e * 64 : j * 128 + e * 64 + 64] = nn(
                vt[e * 64 : e * 64 + 64], pt
            ).astype(bf16)


def attend_first_kernel(
    core_ref, x_ref, mine_ref, other_ref, place_ref, qb_ref, ub_ref,
    qkv_ref, pt_ref, mt_ref, ht_ref, wq_ref, bq_ref, bu_ref, vec_ref,
):
    @pl.when(pl.program_id(0) == 0)
    def _():
        bq_ref[...] = jnp.zeros_like(bq_ref)
        for m in range(2):
            block = jnp.where(core_ref[0] == m, mine_ref[...], other_ref[...])
            w = nn(place_ref[...], block)
            low = w.astype(bf16)
            for t in range(3):
                at = t * D + m * D // 2
                wq_ref[:, at : at + D // 2] = low[:, t * D // 2 : (t + 1) * D // 2]
            small = w[:, 512:640].T
            b = nn(small[64:80].astype(bf16), qb_ref[...])
            bq_ref[:, m * D // 2 : (m + 1) * D // 2] = b[0:1, : D // 2]
            bq_ref[:, 2 * D + m * D // 2 : 2 * D + (m + 1) * D // 2] = b[0:1, D // 2 :]
            u = nn(small[64:80].astype(bf16), ub_ref[...])
            for c in range(2):
                at = m * FF // 2 + c * D
                bu_ref[:, at : at + D] = u[1 + c : 2 + c]
            if m == 0:
                vec_ref[...] = jnp.concatenate(
                    [small[69:71], small[67:68], small[71:73], small[68:69], small[72:74]], 0
                )

    attend_body(x_ref, wq_ref, bq_ref, vec_ref, qkv_ref, pt_ref, mt_ref, ht_ref)


def attend_more_kernel(core_ref, x_ref, wq_ref, bq_ref, vec_ref, a, b, c, d, *outs):
    attend_body(x_ref, wq_ref, bq_ref, vec_ref, *outs)


def attend_outs(n, base):
    specs = [image(s, base) for s in ((1, PAD, 3 * D), (1, 6, PAD, PAD), (1, D, PAD), (1, D, PAD))]
    outs = [
        shape((n, PAD, 3 * D), bf16),
        shape((n, 6, PAD, PAD), bf16),
        shape((n, D, PAD), bf16),
        shape((n, D, PAD), bf16),
    ]
    return outs, specs


def attend_first(core, x, mine, other, place, qb, ub, count):
    outs, specs = attend_outs(x.shape[0], 0)
    square = whole((D, D))
    wide = whole(mine.shape)
    return call(
        attend_first_kernel,
        core,
        count,
        [x, mine, other, place, qb, ub],
        [image((1, PAD, D)), wide, wide, square, square, square],
        outs + [shape((D, 3 * D), bf16), shape((1, 3 * D), f32), shape((1, FF), f32), shape((8, D), f32)],
        specs + [whole((D, 3 * D)), whole((1, 3 * D)), whole((1, FF)), whole((8, D))],
        17,
        name="attend_first",
    )


def attend_more(core, x, wq, bq, vec, done, base):
    outs, specs = attend_outs(x.shape[0], base)
    return call(
        attend_more_kernel,
        core,
        x.shape[0] - base,
        [x, wq, bq, vec, *done],
        [image((1, PAD, D), base), whole((D, 3 * D)), whole((1, 3 * D)), whole((8, D))] + [ANY] * 4,
        outs,
        specs,
        9,
        alias={5: 0, 6: 1, 7: 2, 8: 3},
        name="attend_more",
    )


def feed_kernel(
    core_ref, x_ref, g_ref, mt_ref, mine_ref, other_ref, place_ref, vec_ref, bu_ref,
    out_ref, gres_ref, gm_ref, dw_ref, gcol_ref, gbu_ref,
    wot_ref, wu_ref, wdt_ref, hid_ref, gpl_ref, aco_ref, acu_ref, acd_ref, hat_ref, res_ref, gb_ref,
):
    step = pl.program_id(0)
    last = pl.num_programs(0) - 1
    group = x_ref.shape[0]
    rows = group * PAD
    half = FF // 2

    @pl.when(step == 0)
    def _():
        for m in range(2):
            for a, b, ref, n in ((0, half, wu_ref, half), (half, FF, wdt_ref, half), (FF, FF + D // 2, wot_ref, D // 2)):
                block = jnp.where(core_ref[0] == m, mine_ref[:, a:b], other_ref[:, a:b])
                ref[:, m * n : (m + 1) * n] = nn(place_ref[...], block).astype(bf16)
        aco_ref[...] = jnp.zeros_like(aco_ref)
        acu_ref[...] = jnp.zeros_like(acu_ref)
        acd_ref[...] = jnp.zeros_like(acd_ref)
        gb_ref[...] = jnp.zeros_like(gb_ref)

    bo, gain, shift, bd = [vec_ref[i : i + 1] for i in range(2, 6)]
    x = x_ref[...].reshape(rows, D)
    mixed = jnp.concatenate([mt_ref[i].T for i in range(group)], 0)
    resid = x + nt(mixed, wot_ref[...]) + bo
    res_ref[...] = resid
    hat, inverse = normalise(resid)
    hat_ref[...] = hat
    normed = (hat * gain + shift).astype(bf16)
    glow = g_ref[...].reshape(rows, D).astype(bf16)
    ones = jnp.ones((16, rows), bf16)
    hat_t = jnp.concatenate([hat.astype(bf16).T, ones], 0)
    glow_t = glow.T
    width = 256
    for c in range(0, FF, width):
        cols = slice(c, c + width)
        pre = nn(normed, wu_ref[:, cols]) + bu_ref[:, cols]
        phi = 0.5 + 0.5 * lax.erf(pre * ROOT_HALF)
        slope = phi + pre * (jnp.exp(-0.5 * pre * pre) * INV_ROOT_TAU)
        hid = (pre * phi).astype(bf16)
        hid_ref[:, cols] = hid
        gpl = (nn(glow, wdt_ref[:, cols]) * slope).astype(bf16)
        gpl_ref[:, cols] = gpl
        acd_ref[:, cols] += nn(glow_t, hid)
        acu_ref[:, cols] += nn(hat_t, gpl)
    out = res_ref[...] + nt(hid_ref[...], wdt_ref[...]) + bd
    out_ref[...] = out.astype(bf16).reshape(group, PAD, D)
    gn = nt(gpl_ref[...], wu_ref[...])
    gout = g_ref[...].reshape(rows, D)
    gres = gout + norm_back(gn, hat_ref[...], inverse, gain)
    gres_ref[...] = gres.reshape(group, PAD, D)
    gresl = gres.astype(bf16)
    gb_ref[...] += jnp.sum(gout.reshape(rows // 8, 8, D), axis=0)
    gm_ref[...] = nn(gresl, wot_ref[...]).astype(bf16).reshape(group, PAD, D)
    for i in range(group):
        left = jnp.concatenate([mt_ref[i], ones[:, :PAD]], 0)
        aco_ref[...] += nn(left, gresl[i * PAD : (i + 1) * PAD])

    @pl.when(step == last)
    def _():
        cols = vec_ref[...].T
        gain_c, shift_c = cols[:, 3:4], cols[:, 4:5]
        total = acu_ref[D : D + 1]
        gbu_ref[...] = total
        gg = gs = 0.0
        for m in range(2):
            at = slice(m * half, (m + 1) * half)
            wide = wu_ref[:, at].astype(f32)
            gg = gg + jnp.sum(wide * acu_ref[:D, at], axis=1, keepdims=True)
            gs = gs + jnp.sum(wide * total[:, at], axis=1, keepdims=True)
            dw_ref[m, :, :half] = (acu_ref[:D, at] * gain_c + total[:, at] * shift_c).astype(bf16)
            dw_ref[m, :, half:FF] = acd_ref[:, at].astype(bf16)
        out_t = aco_ref[:D].T.astype(bf16)
        for m in range(2):
            dw_ref[m, :, FF : FF + D // 2] = out_t[:, m * D // 2 : (m + 1) * D // 2]
            dw_ref[m, :, FF + D // 2 :] = jnp.zeros((D, 64), bf16)
        rows_t = jnp.concatenate(
            [aco_ref[D : D + 8], jnp.sum(gb_ref[...], axis=0, keepdims=True), jnp.zeros((7, D), f32)], 0
        ).T
        lane = lax.broadcasted_iota(jnp.int32, (D, 128), 1)
        gcol = jnp.where(lane == 0, rows_t[:, 0:1], 0.0)
        gcol = jnp.where(lane == 1, rows_t[:, 8:9], gcol)
        gcol = jnp.where(lane == 4, gg, gcol)
        gcol_ref[...] = jnp.where(lane == 5, gs, gcol)


def feed(core, x, gout, mt, mine, other, place, vec, bu, group=2):
    n = x.shape[0]
    rows = group * PAD
    img = image((group, PAD, D))
    return call(
        feed_kernel,
        core,
        n // group,
        [x, gout, mt, mine, other, place, vec, bu],
        [img, img, image((group, D, PAD)), whole(mine.shape), whole(mine.shape), whole((D, D)),
         whole((8, D)), whole((1, FF))],
        [shape((n, PAD, D), bf16), shape((n, PAD, D), f32), shape((n, PAD, D), bf16),
         shape((2, D, FF + 256), bf16), shape((D, 128), f32), shape((1, FF), f32)],
        [img, img, img, whole((2, D, FF + 256)), whole((D, 128)), whole((1, FF))],
        43,
        scratch=[
            pltpu.VMEM((D, D), bf16), pltpu.VMEM((D, FF), bf16), pltpu.VMEM((D, FF), bf16),
            pltpu.VMEM((rows, FF), bf16), pltpu.VMEM((rows, FF), bf16),
            pltpu.VMEM((D + 16, D), f32), pltpu.VMEM((D + 16, FF), f32), pltpu.VMEM((D, FF), f32),
            pltpu.VMEM((rows, D), f32), pltpu.VMEM((rows, D), f32), pltpu.VMEM((8, D), f32),
        ],
        name="feed",
    )


def back_kernel(core_ref, gm_ref, qkv_ref, pt_ref, *refs):
    dq_ref, dqt_ref = refs[-2:]
    eighth = jnp.asarray(0.125, bf16)
    lane = lax.broadcasted_iota(jnp.int32, (PAD, 128), 1)
    for j in range(3):
        q = qkv_ref[0, :, j * 128 : j * 128 + 128] * eighth
        kt = (qkv_ref[0, :, D + j * 128 : D + j * 128 + 128] * eighth).T
        v = qkv_ref[0, :, 2 * D + j * 128 : 2 * D + j * 128 + 128]
        do = gm_ref[0, :, j * 128 : j * 128 + 128]
        dk = dv = None
        for e in range(2):
            here = (lane < 64) == (e == 0)
            doh = jnp.where(here, do, jnp.zeros_like(do))
            qh = jnp.where(here, q, jnp.zeros_like(q))
            pt = pt_ref[0, 2 * j + e]
            dvh = nn(pt, doh)
            dp = nt(v, doh)
            p = pt.astype(f32)
            delta = jnp.sum(p * dp, axis=0, keepdims=True)
            ds = (p * (dp - delta)).astype(bf16)
            dkh = nn(ds, qh)
            at = j * 128 + e * 64
            dqt_ref[at : at + 64] = nn(kt[e * 64 : e * 64 + 64], ds).astype(bf16)
            dk = dkh if e == 0 else dk + dkh
            dv = dvh if e == 0 else dv + dvh
        dq_ref[0, :, D + j * 128 : D + j * 128 + 128] = dk.astype(bf16)
        dq_ref[0, :, 2 * D + j * 128 : 2 * D + j * 128 + 128] = dv.astype(bf16)
    dq_ref[0, :, :D] = dqt_ref[...].T


def back(core, gm, qkv, pt, done, base, count):
    more = [] if done is None else [done]
    return call(
        back_kernel,
        core,
        count,
        [gm, qkv, pt] + more,
        [image(s, base) for s in ((1, PAD, D), (1, PAD, 3 * D), (1, 6, PAD, PAD))] + [ANY] * len(more),
        shape(qkv.shape, bf16),
        image((1, PAD, 3 * D), base),
        2 * count,
        scratch=[pltpu.VMEM((D, PAD), bf16)],
        alias={4: 0} if more else None,
        name="back",
    )


def weight_kernel(
    core_ref, ht_ref, dq_ref, wq_ref, vec_ref, gcol_ref, gbu_ref, qb_ref, ub_ref, out_ref, acc_ref
):
    step = pl.program_id(0)

    @pl.when(step == 0)
    def _():
        acc_ref[...] = jnp.zeros_like(acc_ref)

    ones = jnp.ones((16, PAD), bf16)
    for i in range(ht_ref.shape[0]):
        acc_ref[...] += nn(jnp.concatenate([ht_ref[i], ones], 0), dq_ref[i])

    @pl.when(step == pl.num_programs(0) - 1)
    def _():
        cols = vec_ref[...].T
        gain_c, shift_c = cols[:, 0:1], cols[:, 1:2]
        total = acc_ref[D : D + 8]
        lane = lax.broadcasted_iota(jnp.int32, (D, 128), 1)
        gg = gs = 0.0
        for t in range(3):
            at = slice(t * D, (t + 1) * D)
            wide = wq_ref[:, at].astype(f32)
            gg = gg + jnp.sum(wide * acc_ref[:D, at], axis=1, keepdims=True)
            gs = gs + jnp.sum(wide * total[0:1, at], axis=1, keepdims=True)
        gcol = jnp.where(lane == 2, gg, gcol_ref[...])
        gcol = jnp.where(lane == 3, gs, gcol)
        for m in range(2):
            for t in range(3):
                a, b = t * D + m * D // 2, t * D + (m + 1) * D // 2
                dw = acc_ref[:D, a:b] * gain_c + total[0:1, a:b] * shift_c
                out_ref[m, :, t * D // 2 : (t + 1) * D // 2] = dw.astype(bf16)
            row = jnp.concatenate([total[:, m * D // 2 : (m + 1) * D // 2], total[:, 2 * D + m * D // 2 : 2 * D + (m + 1) * D // 2]], 1)
            b = nt(row.astype(bf16), qb_ref[...])
            at = m * FF // 2
            u = jnp.concatenate([gbu_ref[:, at : at + D], gbu_ref[:, at + D : at + 2 * D], jnp.zeros((6, D), f32)], 0)
            u = nt(u.astype(bf16), ub_ref[...])
            extra = jnp.concatenate([b[0:1], u[0:2], jnp.zeros((5, D), f32)], 0).T
            small = jnp.concatenate([extra[:, :3], gcol[:, :6], jnp.zeros((D, 55), f32)], 1)
            out_ref[m, :, 3 * D // 2 :] = small.astype(bf16)


def weight(core, ht, dq, wq, vec, gcol, gbu, qb, ub, group=2):
    n = ht.shape[0]
    return call(
        weight_kernel,
        core,
        n // group,
        [ht, dq, wq, vec, gcol, gbu, qb, ub],
        [image((group, D, PAD)), image((group, PAD, 3 * D)), whole((D, 3 * D)), whole((8, D)),
         whole((D, 128)), whole((1, FF)), whole((D, D)), whole((D, D))],
        shape((2, D, 640), bf16),
        whole((2, D, 640)),
        6,
        scratch=[pltpu.VMEM((D + 16, 3 * D), f32)],
        name="weight",
    )


def inputs_kernel(core_ref, x_ref, gres_ref, dq_ref, wq_ref, vec_ref, *refs):
    out_ref = refs[-1]
    group = x_ref.shape[0]
    rows = group * PAD
    hat, inverse = normalise(x_ref[...].reshape(rows, D))
    gn = nt(dq_ref[...].reshape(rows, 3 * D), wq_ref[...])
    out = gres_ref[...].reshape(rows, D) + norm_back(gn, hat, inverse, vec_ref[0:1])
    out_ref[...] = out.astype(bf16).reshape(group, PAD, D)


def inputs_grad(core, x, gres, dq, wq, vec, done, base, count, group=2):
    more = [] if done is None else [done]
    img = image((group, PAD, D), base // group)
    return call(
        inputs_kernel,
        core,
        count // group,
        [x, gres, dq, wq, vec] + more,
        [img, img, image((group, PAD, 3 * D), base // group), whole((D, 3 * D)), whole((8, D))] + [ANY] * len(more),
        shape(x.shape, bf16),
        img,
        count,
        alias={6: 0} if more else None,
        name="inputs_grad",
    )


def digits(count):
    bits = count.bit_length() - 1
    out = []
    while bits > 0:
        width = 2 if bits % 2 == 0 else 1
        bits -= width
        out.append((bits, width))
    return out


def swap(x, axis, count, mask):
    return lax.ppermute(x, axis, [(i, i ^ mask) for i in range(count)])


def together(*arrays):
    return lax.optimization_barrier(arrays)


def gather_stage(cur, stage, count):
    shift, width = stage
    blocks = [cur] + [swap(cur, "dp", count, d << shift) for d in range(1, 1 << width)]
    return jnp.stack(blocks).reshape((-1,) + cur.shape[1:])


def gathered_from(stages):
    masks = np.zeros(1, np.int32)
    for shift, width in stages:
        masks = np.concatenate([masks ^ (d << shift) for d in range(1 << width)])
    return masks


def scatter_stage(cur, stage, count, last):
    me = lax.axis_index("dp")
    shift, width = stage
    radix = 1 << width
    cur = cur.reshape((-1, radix) + cur.shape[-2:])
    digit = (me >> shift) & (radix - 1)
    total = lax.dynamic_index_in_dim(cur, digit, 1, False).astype(f32)
    for d in range(1, radix):
        part = lax.dynamic_index_in_dim(cur, digit ^ d, 1, False)
        total = total + swap(part, "dp", count, d << shift).astype(f32)
    return total if last else total.astype(bf16)


def permutation(count, parts, size):
    to = np.arange(count * parts * size).reshape(parts, count, size).transpose(1, 0, 2).reshape(-1)
    cols = lax.broadcasted_iota(jnp.int32, (D, D), 1)
    return (jnp.asarray(to, jnp.int32)[:, None] == cols).astype(bf16)


def per_device(dp, *args):
    (inputs, w_qkv, b_qv, w_out, b_out, w_up, b_up, w_down, b_down, g1, s1, g2, s2, grad_out) = args
    core_id = lax.axis_index("mp")
    core = core_id.astype(jnp.int32)[None]
    me = lax.axis_index("dp")
    share = D // dp
    stages = digits(dp)

    small = [b_qv.reshape(1, share), b_up.reshape(2, share)]
    small += [v[None] for v in (b_out, b_down, g1, s1, g2, s2)]
    small = jnp.concatenate(small).T
    first = [w_qkv[t] for t in range(3)] + [small, jnp.zeros((share, 55), bf16)]
    first = jnp.concatenate(first, 1)[None]
    rest = [w_up, w_down.T, w_out.T, jnp.zeros((share, 64), bf16)]
    rest = jnp.concatenate(rest, 1)[None]

    source = me ^ jnp.asarray(np.repeat(gathered_from(stages), share))
    inner = np.tile(np.arange(share), dp)
    outer = np.repeat(np.arange(dp), share)
    place = (outer[:, None] == source[None]) & (inner[:, None] == inner[None])
    place = place.astype(bf16)
    qb = permutation(dp, 6, b_qv.shape[2])
    ub = permutation(dp, 3, b_up.shape[1])

    first = gather_stage(first, stages[0], dp)
    first, rest, x = together(first, rest, prepare(core, inputs))
    rest = gather_stage(rest, stages[0], dp)
    for stage in stages[1:]:
        first = gather_stage(first, stage, dp)
    first, gout = together(first.reshape(D, -1), prepare(core, grad_out))
    first_other, rest = together(swap(first, "mp", 2, 1), rest)
    for stage in stages[1:]:
        rest = gather_stage(rest, stage, dp)
    n_a = 8
    *done, wq, bq, bu, vec = attend_first(core, x, first, first_other, place, qb, ub, n_a)
    wq, rest = together(wq, rest.reshape(D, -1))
    rest_other = swap(rest, "mp", 2, 1)
    qkv, pts, mixed_t, hat_t = attend_more(core, x, wq, bq, vec, done, n_a)

    output, gres, gmixed, grest, gcol, gbu = feed(
        core, x, gout, mixed_t, rest, rest_other, place, vec, bu
    )

    def reduce_cores(g):
        own = lax.dynamic_index_in_dim(g, core_id, 0, False)
        give = lax.dynamic_index_in_dim(g, 1 - core_id, 0, False)
        total = own.astype(f32) + swap(give, "mp", 2, 1).astype(f32)
        return total.astype(bf16).reshape(dp, share, -1)

    back_stages = stages[::-1]

    def scatter_on(g, index):
        return scatter_stage(g, back_stages[index], dp, index == len(back_stages) - 1)

    grest = reduce_cores(grest)
    output_other = swap(output, "mp", 2, 1)
    cuts = [0, 3, 8, 12]
    dqkv = back(core, gmixed, qkv, pts, None, 0, cuts[1])
    dqkv, grest = together(dqkv, grest)
    grest = scatter_on(grest, 0)
    dqkv = back(core, gmixed, qkv, pts, dqkv, cuts[1], cuts[2] - cuts[1])
    dqkv, grest, output_other = together(dqkv, grest, output_other)
    for i in range(1, len(back_stages)):
        grest = scatter_on(grest, i)
    dqkv = back(core, gmixed, qkv, pts, dqkv, cuts[2], cuts[3] - cuts[2])
    dqkv, grest = together(dqkv, grest)

    gfirst = weight(core, hat_t, dqkv, wq, vec, gcol, gbu, qb, ub)
    gfirst, dqkv = together(gfirst, dqkv)
    gfirst = reduce_cores(gfirst)
    gin = inputs_grad(core, x, gres, dqkv, wq, vec, None, 0, 4)
    gin, gfirst = together(gin, gfirst)
    gfirst = scatter_on(gfirst, 0)
    gin = inputs_grad(core, x, gres, dqkv, wq, vec, gin, 4, 8)
    gin, gfirst = together(gin, gfirst)
    gin_other = swap(gin, "mp", 2, 1)
    for i in range(1, len(back_stages)):
        gfirst = scatter_on(gfirst, i)
    out_full = join(core, output, output_other)
    gin_full = join(core, gin, gin_other)

    gfirst, grest = gfirst[0], grest[0]
    n_q, n_u = w_qkv.shape[2], w_up.shape[1]
    tail = gfirst[:, 3 * n_q : 3 * n_q + 9].T
    gbo, gbd, gg1, gs1, gg2, gs2 = [tail[i] for i in range(3, 9)]
    gw_qkv = jnp.stack([gfirst[:, t * n_q : (t + 1) * n_q] for t in range(3)])
    return (
        out_full,
        gin_full,
        gw_qkv,
        tail[0].reshape(b_qv.shape),
        grest[:, 2 * n_u : 2 * n_u + w_out.shape[0]].T,
        gbo,
        grest[:, :n_u],
        tail[1:3].reshape(b_up.shape),
        grest[:, n_u : 2 * n_u].T,
        gbd,
        gg1,
        gs1,
        gg2,
        gs2,
    )


def solution(mesh):
    specs = (
        P("dp", None),
        P(None, "dp", "mp"),
        P(None, "mp", "dp"),
        P("mp", "dp"),
        P("dp"),
        P("dp", "mp"),
        P("mp", "dp"),
        P("mp", "dp"),
        P("dp"),
        P("dp"),
        P("dp"),
        P("dp"),
        P("dp"),
    )
    dp = mesh.shape["dp"]

    def run(*args):
        return per_device(dp, *args)

    return jax.shard_map(
        run,
        mesh=mesh,
        in_specs=specs + (P("dp", None),),
        out_specs=(P("dp", None),) + specs,
        check_vma=False,
    )
```

```python
import jax
import jax.numpy as jnp
import numpy as np
from jax import lax
from jax.experimental import pallas as pl
from jax.experimental.pallas import tpu as pltpu
from jax.sharding import PartitionSpec as P

HEAD_DIM = 64
SEQ = 197
PAD = 208
EPS = 1e-06
ROOT_HALF = 0.7071067811865476
INV_ROOT_TAU = 0.3989422804014327
D = 384
FF = 1536


f32 = jnp.float32
bf16 = jnp.bfloat16


def nt(a, b):
    return lax.dot_general(a, b, (((1,), (1,)), ((), ())), preferred_element_type=f32)


def nn(a, b):
    return lax.dot_general(a, b, (((1,), (0,)), ((), ())), preferred_element_type=f32)


def normalise(x):
    center = x - jnp.mean(x, axis=-1, keepdims=True)
    inverse = lax.rsqrt(jnp.mean(center * center, axis=-1, keepdims=True) + EPS)
    return center * inverse, inverse


def norm_back(grad, hat, inverse, gain):
    scaled = grad * gain
    first = jnp.mean(scaled, axis=-1, keepdims=True)
    second = jnp.mean(scaled * hat, axis=-1, keepdims=True)
    return inverse * (scaled - first - hat * second)


LIMIT = 60 * 1024 * 1024
ANY = pl.BlockSpec(memory_space=pl.ANY)


def whole(shape):
    return pl.BlockSpec(shape, lambda i, *_: (0,) * len(shape))


def image(shape, base=0):
    return pl.BlockSpec(shape, lambda i, *_: (i + base,) + (0,) * (len(shape) - 1))


def call(kernel, core, grid, ins, in_specs, outs, out_specs, cost, scratch=(), alias=None, name=None):
    return pl.pallas_call(
        kernel,
        grid_spec=pltpu.PrefetchScalarGridSpec(
            num_scalar_prefetch=1,
            grid=(grid,),
            in_specs=in_specs,
            out_specs=out_specs,
            scratch_shapes=list(scratch),
        ),
        out_shape=outs,
        input_output_aliases=alias or {},
        compiler_params=pltpu.CompilerParams(vmem_limit_bytes=LIMIT),
        cost_estimate=pl.CostEstimate(
            flops=cost * 10**9 // 4, bytes_accessed=cost * 3 * 10**6, transcendentals=0
        ),
        name=name,
    )(core, *ins)


def shape(dims, dtype):
    return jax.ShapeDtypeStruct(dims, dtype)


def prepare_kernel(rows, group, core_ref, *refs):
    out_ref = refs[-1]
    sub = lax.broadcasted_iota(jnp.int32, (PAD // 8, 8, D), 1)
    row = lax.broadcasted_iota(jnp.int32, (PAD, D), 0)
    for k in range(group):
        at = SEQ * (pl.program_id(0) * group + k + core_ref[0] * (rows // (2 * SEQ)))
        off = at - first_row(at, rows)
        x = refs[k][...].reshape(PAD // 8, 8, D)
        x = jnp.where(off >= 8, jnp.concatenate([x[1:], x[:1]], 0), x)
        rest = lax.rem(off, 8)
        x = pltpu.roll(x, lax.rem(8 - rest, 8), 1)
        x = jnp.where(sub < 8 - rest, x, jnp.concatenate([x[1:], x[:1]], 0))
        out_ref[k] = jnp.where(row < SEQ, x.reshape(PAD, D), 0.0)


def first_row(at, rows):
    return jnp.minimum(at // 8, (rows - PAD) // 8) * 8


def prepare(core, a, group=2):
    rows = a.shape[0]
    images = rows // (2 * SEQ)

    def spec(k):
        def at(i, core):
            row = first_row(SEQ * (i * group + k + core[0] * images), rows)
            return pl.multiple_of(row, 8), 0

        return pl.BlockSpec((pl.Element(PAD), pl.Element(D)), at)

    return call(
        lambda *r: prepare_kernel(rows, group, *r),
        core,
        images // group,
        [a] * group,
        [spec(k) for k in range(group)],
        shape((images, PAD, D), f32),
        image((group, PAD, D)),
        4,
        name="prepare",
    )


def join_kernel(images, core_ref, mine_ref, other_ref, out_ref, buf, sem):
    step = pl.program_id(0)
    core = core_ref[0]

    @pl.when(step == 0)
    def _():
        for g in range(2 * images):
            @pl.when(core == g // images)
            def _():
                pltpu.make_async_copy(mine_ref.at[g % images], buf.at[g], sem.at[g]).start()

            @pl.when(core != g // images)
            def _():
                pltpu.make_async_copy(other_ref.at[g % images], buf.at[g], sem.at[g]).start()

    for k in range(8):
        g = 8 * step + k
        pltpu.make_async_copy(mine_ref.at[0], buf.at[g], sem.at[g]).wait()
        out_ref[SEQ * k : SEQ * k + SEQ, :] = buf[g, :SEQ, :].astype(f32)


def join(core, mine, other):
    images = mine.shape[0]
    return call(
        lambda *r: join_kernel(images, *r),
        core,
        2 * images // 8,
        [mine, other],
        [ANY, ANY],
        shape((2 * images * SEQ, D), f32),
        pl.BlockSpec((8 * SEQ, D), lambda i, _: (i, 0)),
        5,
        scratch=[pltpu.VMEM((2 * images, PAD, D), bf16), pltpu.SemaphoreType.DMA((2 * images,))],
        name="join",
    )


HEADS = 6
G = 2
AHEAD = 3


def weave(long, short):
    at = [(k + 1) * len(long) // (len(short) + 1) for k in range(len(short))]
    for n, step in enumerate(long):
        for k, s in enumerate(short):
            if at[k] == n:
                s()
        step()


def qkv_steps(x_ref, wq_ref, bq_ref, vec_ref, qkv_ref, ht_ref):
    state = {}
    rows = G * PAD

    def norm():
        hat, _ = normalise(x_ref[...].reshape(rows, D))
        low = hat.astype(bf16)
        for i in range(G):
            ht_ref[i] = low[i * PAD : (i + 1) * PAD].T
        state["n"] = (hat * vec_ref[0:1] + vec_ref[1:2]).astype(bf16)

    def project(a, b):
        qkv_ref[:, :, a:b] = (
            (nn(state["n"], wq_ref[:, a:b]) + bq_ref[:, a:b]).astype(bf16).reshape(G, PAD, b - a)
        )

    cuts = list(range(0, 3 * D, 256)) + [3 * D]
    return [norm] + [lambda a=a, b=b: project(a, b) for a, b in zip(cuts, cuts[1:])]


def attention_steps(qkv_ref, i, st_ref, pt_ref, mt_ref):
    lane = lax.broadcasted_iota(jnp.int32, (PAD, 128), 1)
    tail = lax.broadcasted_iota(jnp.int32, (16, PAD), 0) < SEQ - (PAD - 16)
    vts = {}

    def score(h):
        j, e = divmod(h, 2)
        q = qkv_ref[:, j * 128 : j * 128 + 128] * jnp.asarray(0.125, bf16)
        k = qkv_ref[:, D + j * 128 : D + j * 128 + 128]
        st_ref[h % (AHEAD + 1)] = nt(jnp.where((lane < 64) == (e == 0), k, jnp.zeros_like(k)), q)

    def soften(h):
        st = st_ref[h % (AHEAD + 1)]
        body, end = st[: PAD - 16], jnp.where(tail, st[PAD - 16 :], -1e30)
        st = jnp.concatenate([body, end], 0)
        top = jnp.max(st, axis=0, keepdims=True)
        ex = jnp.exp(st - top)
        total = jnp.sum(ex, axis=0, keepdims=True)
        pt_ref[i, h] = (ex * (1.0 / total)).astype(bf16)

    def mix(h):
        j, e = divmod(h, 2)
        if j not in vts:
            vts[j] = qkv_ref[:, 2 * D + j * 128 : 2 * D + j * 128 + 128].T
        mt_ref[i, h * 64 : h * 64 + 64] = nn(
            vts[j][e * 64 : e * 64 + 64], pt_ref[i, h]
        ).astype(bf16)

    def start():
        for h in range(AHEAD):
            score(h)

    def step(h):
        if h + AHEAD < HEADS:
            score(h + AHEAD)
        soften(h)
        if h > 0:
            mix(h - 1)
        if h == HEADS - 1:
            mix(h)

    return [start] + [lambda h=h: step(h) for h in range(HEADS)]


def attend_body(
    x_ref, next_ref, wq_ref, bq_ref, vec_ref, qkv_ref, pt_ref, mt_ref, ht_ref,
    now_ref, next_qkv_ref, next_ht_ref, st_ref,
):
    @pl.when(pl.program_id(0) == 0)
    def _():
        for s in qkv_steps(x_ref, wq_ref, bq_ref, vec_ref, next_qkv_ref, next_ht_ref):
            s()

    ht_ref[...] = next_ht_ref[...]
    steps = []
    for i in range(G):
        now_ref[i] = next_qkv_ref[i]
        qkv_ref[i] = next_qkv_ref[i]
        steps += attention_steps(now_ref.at[i], i, st_ref, pt_ref, mt_ref)
    weave(steps, qkv_steps(next_ref, wq_ref, bq_ref, vec_ref, next_qkv_ref, next_ht_ref))


def attend_first_kernel(
    core_ref, x_ref, next_ref, mine_ref, other_ref, place_ref, qb_ref, ub_ref,
    qkv_ref, pt_ref, mt_ref, ht_ref, wq_ref, bq_ref, bu_ref, vec_ref, *scratch,
):
    @pl.when(pl.program_id(0) == 0)
    def _():
        bq_ref[...] = jnp.zeros_like(bq_ref)
        for m in range(2):
            block = jnp.where(core_ref[0] == m, mine_ref[...], other_ref[...])
            w = nn(place_ref[...], block)
            low = w.astype(bf16)
            for t in range(3):
                at = t * D + m * D // 2
                wq_ref[:, at : at + D // 2] = low[:, t * D // 2 : (t + 1) * D // 2]
            small = w[:, 512:640].T
            b = nn(small[64:80].astype(bf16), qb_ref[...])
            bq_ref[:, m * D // 2 : (m + 1) * D // 2] = b[0:1, : D // 2]
            bq_ref[:, 2 * D + m * D // 2 : 2 * D + (m + 1) * D // 2] = b[0:1, D // 2 :]
            u = nn(small[64:80].astype(bf16), ub_ref[...])
            for c in range(2):
                at = m * FF // 2 + c * D
                bu_ref[:, at : at + D] = u[1 + c : 2 + c]
            if m == 0:
                vec_ref[...] = jnp.concatenate(
                    [small[69:71], small[67:68], small[71:73], small[68:69], small[72:74]], 0
                )

    attend_body(
        x_ref, next_ref, wq_ref, bq_ref, vec_ref, qkv_ref, pt_ref, mt_ref, ht_ref, *scratch
    )


def attend_more_kernel(core_ref, x_ref, next_ref, wq_ref, bq_ref, vec_ref, a, b, c, d, *outs):
    attend_body(x_ref, next_ref, wq_ref, bq_ref, vec_ref, *outs)


def attend_outs(n, base):
    dims = (PAD, 3 * D), (6, PAD, PAD), (D, PAD), (D, PAD)
    return [shape((n, *d), bf16) for d in dims], [image((G, *d), base) for d in dims]


def attend_ins(base, count):
    first = pl.BlockSpec((G, PAD, D), lambda i, *_: (base, 0, 0))
    later = pl.BlockSpec((G, PAD, D), lambda i, *_: (base + jnp.minimum(i + 1, count - 1), 0, 0))
    return [first, later]


def attend_scratch():
    return [
        pltpu.VMEM((G, PAD, 3 * D), bf16),
        pltpu.VMEM((G, PAD, 3 * D), bf16),
        pltpu.VMEM((G, D, PAD), bf16),
        pltpu.VMEM((AHEAD + 1, PAD, PAD), f32),
    ]


def attend_first(core, x, mine, other, place, qb, ub, count):
    outs, specs = attend_outs(x.shape[0], 0)
    square = whole((D, D))
    wide = whole(mine.shape)
    outs += [shape((D, 3 * D), bf16), shape((1, 3 * D), f32), shape((1, FF), f32), shape((8, D), f32)]
    return call(
        attend_first_kernel,
        core,
        count,
        [x, x, mine, other, place, qb, ub],
        attend_ins(0, count) + [wide, wide, square, square, square],
        outs,
        specs + [whole(o.shape) for o in outs[4:]],
        3 * count,
        scratch=attend_scratch(),
        name="attend_first",
    )


def attend_more(core, x, wq, bq, vec, done, base):
    outs, specs = attend_outs(x.shape[0], base)
    count = x.shape[0] // G - base
    return call(
        attend_more_kernel,
        core,
        count,
        [x, x, wq, bq, vec, *done],
        attend_ins(base, count) + [whole(a.shape) for a in (wq, bq, vec)] + [ANY] * 4,
        outs,
        specs,
        3 * count,
        scratch=attend_scratch(),
        alias={6: 0, 7: 1, 8: 2, 9: 3},
        name="attend_more",
    )


def feed_kernel(
    core_ref, x_ref, g_ref, mt_ref, mine_ref, other_ref, place_ref, vec_ref, bu_ref,
    out_ref, gres_ref, gm_ref, dw_ref, gcol_ref, gbu_ref,
    wot_ref, wu_ref, wdt_ref, hid_ref, gpl_ref, aco_ref, acu_ref, acd_ref, hat_ref, res_ref, gb_ref,
):
    step = pl.program_id(0)
    last = pl.num_programs(0) - 1
    group = x_ref.shape[0]
    rows = group * PAD
    half = FF // 2

    @pl.when(step == 0)
    def _():
        for m in range(2):
            for a, b, ref, n in ((0, half, wu_ref, half), (half, FF, wdt_ref, half), (FF, FF + D // 2, wot_ref, D // 2)):
                block = jnp.where(core_ref[0] == m, mine_ref[:, a:b], other_ref[:, a:b])
                ref[:, m * n : (m + 1) * n] = nn(place_ref[...], block).astype(bf16)
        aco_ref[...] = jnp.zeros_like(aco_ref)
        acu_ref[...] = jnp.zeros_like(acu_ref)
        acd_ref[...] = jnp.zeros_like(acd_ref)
        gb_ref[...] = jnp.zeros_like(gb_ref)

    bo, gain, shift, bd = [vec_ref[i : i + 1] for i in range(2, 6)]
    x = x_ref[...].reshape(rows, D)
    mixed = jnp.concatenate([mt_ref[i].T for i in range(group)], 0)
    resid = x + nt(mixed, wot_ref[...]) + bo
    res_ref[...] = resid
    hat, inverse = normalise(resid)
    hat_ref[...] = hat
    normed = (hat * gain + shift).astype(bf16)
    glow = g_ref[...].reshape(rows, D).astype(bf16)
    ones = jnp.ones((16, rows), bf16)
    hat_t = jnp.concatenate([hat.astype(bf16).T, ones], 0)
    glow_t = glow.T
    width = 256
    for c in range(0, FF, width):
        cols = slice(c, c + width)
        pre = nn(normed, wu_ref[:, cols]) + bu_ref[:, cols]
        phi = 0.5 + 0.5 * lax.erf(pre * ROOT_HALF)
        slope = phi + pre * (jnp.exp(-0.5 * pre * pre) * INV_ROOT_TAU)
        hid = (pre * phi).astype(bf16)
        hid_ref[:, cols] = hid
        gpl = (nn(glow, wdt_ref[:, cols]) * slope).astype(bf16)
        gpl_ref[:, cols] = gpl
        acd_ref[:, cols] += nn(glow_t, hid)
        acu_ref[:, cols] += nn(hat_t, gpl)
    out = res_ref[...] + nt(hid_ref[...], wdt_ref[...]) + bd
    out_ref[...] = out.astype(bf16).reshape(group, PAD, D)
    gn = nt(gpl_ref[...], wu_ref[...])
    gout = g_ref[...].reshape(rows, D)
    gres = gout + norm_back(gn, hat_ref[...], inverse, gain)
    gres_ref[...] = gres.reshape(group, PAD, D)
    gresl = gres.astype(bf16)
    gb_ref[...] += jnp.sum(gout.reshape(rows // 8, 8, D), axis=0)
    gm_ref[...] = nn(gresl, wot_ref[...]).astype(bf16).reshape(group, PAD, D)
    for i in range(group):
        left = jnp.concatenate([mt_ref[i], ones[:, :PAD]], 0)
        aco_ref[...] += nn(left, gresl[i * PAD : (i + 1) * PAD])

    @pl.when(step == last)
    def _():
        cols = vec_ref[...].T
        gain_c, shift_c = cols[:, 3:4], cols[:, 4:5]
        total = acu_ref[D : D + 1]
        gbu_ref[...] = total
        gg = gs = 0.0
        for m in range(2):
            at = slice(m * half, (m + 1) * half)
            wide = wu_ref[:, at].astype(f32)
            gg = gg + jnp.sum(wide * acu_ref[:D, at], axis=1, keepdims=True)
            gs = gs + jnp.sum(wide * total[:, at], axis=1, keepdims=True)
            dw_ref[m, :, :half] = (acu_ref[:D, at] * gain_c + total[:, at] * shift_c).astype(bf16)
            dw_ref[m, :, half:FF] = acd_ref[:, at].astype(bf16)
        out_t = aco_ref[:D].T.astype(bf16)
        for m in range(2):
            dw_ref[m, :, FF : FF + D // 2] = out_t[:, m * D // 2 : (m + 1) * D // 2]
            dw_ref[m, :, FF + D // 2 :] = jnp.zeros((D, 64), bf16)
        rows_t = jnp.concatenate(
            [aco_ref[D : D + 8], jnp.sum(gb_ref[...], axis=0, keepdims=True), jnp.zeros((7, D), f32)], 0
        ).T
        lane = lax.broadcasted_iota(jnp.int32, (D, 128), 1)
        gcol = jnp.where(lane == 0, rows_t[:, 0:1], 0.0)
        gcol = jnp.where(lane == 1, rows_t[:, 8:9], gcol)
        gcol = jnp.where(lane == 4, gg, gcol)
        gcol_ref[...] = jnp.where(lane == 5, gs, gcol)


def feed(core, x, gout, mt, mine, other, place, vec, bu, group=2):
    n = x.shape[0]
    rows = group * PAD
    img = image((group, PAD, D))
    return call(
        feed_kernel,
        core,
        n // group,
        [x, gout, mt, mine, other, place, vec, bu],
        [img, img, image((group, D, PAD)), whole(mine.shape), whole(mine.shape), whole((D, D)),
         whole((8, D)), whole((1, FF))],
        [shape((n, PAD, D), bf16), shape((n, PAD, D), f32), shape((n, PAD, D), bf16),
         shape((2, D, FF + 256), bf16), shape((D, 128), f32), shape((1, FF), f32)],
        [img, img, img, whole((2, D, FF + 256)), whole((D, 128)), whole((1, FF))],
        43,
        scratch=[
            pltpu.VMEM((D, D), bf16), pltpu.VMEM((D, FF), bf16), pltpu.VMEM((D, FF), bf16),
            pltpu.VMEM((rows, FF), bf16), pltpu.VMEM((rows, FF), bf16),
            pltpu.VMEM((D + 16, D), f32), pltpu.VMEM((D + 16, FF), f32), pltpu.VMEM((D, FF), f32),
            pltpu.VMEM((rows, D), f32), pltpu.VMEM((rows, D), f32), pltpu.VMEM((8, D), f32),
        ],
        name="feed",
    )


BACK_AHEAD = 2


def back_steps(gm_ref, qkv_ref, pt_ref, i, dq_ref, dp_ref, ds_ref, dqt_ref):
    eighth = jnp.asarray(0.125, bf16)
    lane = lax.broadcasted_iota(jnp.int32, (PAD, 128), 1)
    kts = {}

    def cols(t, h):
        at = t * D + h // 2 * 128
        return slice(at, at + 128)

    def pre(h):
        do = gm_ref[i, :, cols(0, h)]
        do = jnp.where((lane < 64) == (h % 2 == 0), do, jnp.zeros_like(do))
        dp_ref[h % (BACK_AHEAD + 1)] = nt(qkv_ref[i, :, cols(2, h)], do)

    def mid(h):
        dp = dp_ref[h % (BACK_AHEAD + 1)]
        p = pt_ref[i, h].astype(f32)
        delta = jnp.sum(p * dp, axis=0, keepdims=True)
        ds_ref[h % 2] = (p * (dp - delta)).astype(bf16)

    def keep(t, h, value):
        e = h % 2
        at = t * D + h * 64
        dq_ref[i, :, at : at + 64] = value[:, e * 64 : e * 64 + 64].astype(bf16)

    def post(h):
        j, e = divmod(h, 2)
        if j not in kts:
            kts[j] = (qkv_ref[i, :, cols(1, h)] * eighth).T
        ds = ds_ref[h % 2]
        keep(1, h, nn(ds, qkv_ref[i, :, cols(0, h)] * eighth))
        keep(2, h, nn(pt_ref[i, h], gm_ref[i, :, cols(0, h)]))
        dqt_ref[h * 64 : h * 64 + 64] = nn(kts[j][e * 64 : e * 64 + 64], ds).astype(bf16)

    def start():
        for h in range(BACK_AHEAD):
            pre(h)

    def step(h):
        if h + BACK_AHEAD < HEADS:
            pre(h + BACK_AHEAD)
        mid(h)
        if h > 0:
            post(h - 1)
        if h == HEADS - 1:
            post(h)
            dq_ref[i, :, :D] = dqt_ref[...].T

    return [start] + [lambda h=h: step(h) for h in range(HEADS)]


def back_kernel(begin, end, core_ref, gm_ref, qkv_ref, pt_ref, ht_ref, *refs):
    dp_ref, ds_ref, dqt_ref = refs[-3:]
    refs = list(refs[:-3])
    if not begin:
        acc_in, old_in, _ = [refs.pop(0) for _ in range(3)]
    if end:
        final_ht, wq_ref, vec_ref, gcol_ref, gbu_ref, qb_ref, ub_ref = [refs.pop(0) for _ in range(7)]
        dq_ref, acc_ref, old_ref, pack_ref = refs
    else:
        dq_ref, acc_ref, old_ref = refs
    step = pl.program_id(0)

    @pl.when(step == 0)
    def _():
        acc_ref[...] = jnp.zeros_like(acc_ref) if begin else acc_in[...]
        old_ref[...] = jnp.zeros_like(old_ref) if begin else old_in[...]

    ones = jnp.ones((16, PAD), bf16)

    def add(ht, dq, i, a):
        left = jnp.concatenate([ht[i], ones], 0)
        acc_ref[:, a : a + 384] += nn(left, dq[i, :, a : a + 384])

    blocks = [(i, a) for i in range(G) for a in range(0, 3 * D, 384)]
    steps = []
    for i in range(G):
        steps += back_steps(gm_ref, qkv_ref, pt_ref, i, dq_ref, dp_ref, ds_ref, dqt_ref)
    weave(steps, [lambda i=i, a=a: add(ht_ref, old_ref, i, a) for i, a in blocks])
    old_ref[...] = dq_ref[...]

    if end:

        @pl.when(step == pl.num_programs(0) - 1)
        def _():
            for i, a in blocks:
                add(final_ht, dq_ref, i, a)
            finish(acc_ref, wq_ref, vec_ref, gcol_ref, gbu_ref, qb_ref, ub_ref, pack_ref)


def finish(acc_ref, wq_ref, vec_ref, gcol_ref, gbu_ref, qb_ref, ub_ref, out_ref):
    cols = vec_ref[...].T
    gain_c, shift_c = cols[:, 0:1], cols[:, 1:2]
    total = acc_ref[D : D + 8]
    lane = lax.broadcasted_iota(jnp.int32, (D, 128), 1)
    gg = gs = 0.0
    for t in range(3):
        at = slice(t * D, (t + 1) * D)
        wide = wq_ref[:, at].astype(f32)
        gg = gg + jnp.sum(wide * acc_ref[:D, at], axis=1, keepdims=True)
        gs = gs + jnp.sum(wide * total[0:1, at], axis=1, keepdims=True)
    gcol = jnp.where(lane == 2, gg, gcol_ref[...])
    gcol = jnp.where(lane == 3, gs, gcol)
    for m in range(2):
        q, v = m * D // 2, 2 * D + m * D // 2
        for t in range(3):
            a, b = t * D + m * D // 2, t * D + (m + 1) * D // 2
            dw = acc_ref[:D, a:b] * gain_c + total[0:1, a:b] * shift_c
            out_ref[m, :, t * D // 2 : (t + 1) * D // 2] = dw.astype(bf16)
        row = jnp.concatenate([total[:, q : q + D // 2], total[:, v : v + D // 2]], 1)
        b = nt(row.astype(bf16), qb_ref[...])
        at = m * FF // 2
        u = [gbu_ref[:, at : at + D], gbu_ref[:, at + D : at + 2 * D], jnp.zeros((6, D), f32)]
        u = nt(jnp.concatenate(u, 0).astype(bf16), ub_ref[...])
        extra = jnp.concatenate([b[0:1], u[0:2], jnp.zeros((5, D), f32)], 0).T
        small = jnp.concatenate([extra[:, :3], gcol[:, :6], jnp.zeros((D, 55), f32)], 1)
        out_ref[m, :, 3 * D // 2 :] = small.astype(bf16)


def back(core, gm, qkv, pt, ht, state, base, count, final=None):
    begin, end = state is None, final is not None
    ins = [gm, qkv, pt, ht]
    specs = [image(s, base) for s in ((G, PAD, D), (G, PAD, 3 * D), (G, 6, PAD, PAD))]
    specs.append(pl.BlockSpec((G, D, PAD), lambda i, *_: (jnp.maximum(i + base - 1, 0), 0, 0)))
    outs = [shape(qkv.shape, bf16), shape((D + 16, 3 * D), f32), shape((G, PAD, 3 * D), bf16)]
    out_specs = [image((G, PAD, 3 * D), base), whole(outs[1].shape), whole(outs[2].shape)]
    alias = {}
    if not begin:
        ins += [state[1], state[2], state[0]]
        specs += [whole(outs[1].shape), whole(outs[2].shape), ANY]
        alias = {7: 0}
    if end:
        ins += [ht, *final]
        specs.append(pl.BlockSpec((G, D, PAD), lambda i, *_: (base + count - 1, 0, 0)))
        specs += [whole(a.shape) for a in final]
        outs.append(shape((2, D, 640), bf16))
        out_specs.append(whole((2, D, 640)))
    return call(
        lambda *r: back_kernel(begin, end, *r),
        core,
        count,
        ins,
        specs,
        outs,
        out_specs,
        4 * count,
        scratch=[pltpu.VMEM(((BACK_AHEAD + 1), PAD, PAD), f32), pltpu.VMEM((2, PAD, PAD), bf16), pltpu.VMEM((D, PAD), bf16)],
        alias=alias,
        name="back",
    )


def inputs_kernel(core_ref, x_ref, gres_ref, dq_ref, wq_ref, vec_ref, *refs):
    out_ref = refs[-1]
    group = x_ref.shape[0]
    rows = group * PAD
    hat, inverse = normalise(x_ref[...].reshape(rows, D))
    gn = nt(dq_ref[...].reshape(rows, 3 * D), wq_ref[...])
    out = gres_ref[...].reshape(rows, D) + norm_back(gn, hat, inverse, vec_ref[0:1])
    out_ref[...] = out.astype(bf16).reshape(group, PAD, D)


def inputs_grad(core, x, gres, dq, wq, vec, done, base, count, group=2):
    more = [] if done is None else [done]
    img = image((group, PAD, D), base // group)
    return call(
        inputs_kernel,
        core,
        count // group,
        [x, gres, dq, wq, vec] + more,
        [img, img, image((group, PAD, 3 * D), base // group), whole((D, 3 * D)), whole((8, D))] + [ANY] * len(more),
        shape(x.shape, bf16),
        img,
        count,
        alias={6: 0} if more else None,
        name="inputs_grad",
    )


def digits(count):
    bits = count.bit_length() - 1
    out = []
    while bits > 0:
        width = 2 if bits % 2 == 0 else 1
        bits -= width
        out.append((bits, width))
    return out


def swap(x, axis, count, mask):
    return lax.ppermute(x, axis, [(i, i ^ mask) for i in range(count)])


def together(*arrays):
    return lax.optimization_barrier(arrays)


def gather_stage(cur, stage, count):
    shift, width = stage
    blocks = [cur] + [swap(cur, "dp", count, d << shift) for d in range(1, 1 << width)]
    return jnp.stack(blocks).reshape((-1,) + cur.shape[1:])


def gathered_from(stages):
    masks = np.zeros(1, np.int32)
    for shift, width in stages:
        masks = np.concatenate([masks ^ (d << shift) for d in range(1 << width)])
    return masks


def scatter_stage(cur, stage, count, last):
    me = lax.axis_index("dp")
    shift, width = stage
    radix = 1 << width
    cur = cur.reshape((-1, radix) + cur.shape[-2:])
    digit = (me >> shift) & (radix - 1)
    total = lax.dynamic_index_in_dim(cur, digit, 1, False).astype(f32)
    for d in range(1, radix):
        part = lax.dynamic_index_in_dim(cur, digit ^ d, 1, False)
        total = total + swap(part, "dp", count, d << shift).astype(f32)
    return total if last else total.astype(bf16)


def permutation(count, parts, size):
    to = np.arange(count * parts * size).reshape(parts, count, size).transpose(1, 0, 2).reshape(-1)
    cols = lax.broadcasted_iota(jnp.int32, (D, D), 1)
    return (jnp.asarray(to, jnp.int32)[:, None] == cols).astype(bf16)


def per_device(dp, *args):
    (inputs, w_qkv, b_qv, w_out, b_out, w_up, b_up, w_down, b_down, g1, s1, g2, s2, grad_out) = args
    core_id = lax.axis_index("mp")
    core = core_id.astype(jnp.int32)[None]
    me = lax.axis_index("dp")
    share = D // dp
    stages = digits(dp)

    small = [b_qv.reshape(1, share), b_up.reshape(2, share)]
    small += [v[None] for v in (b_out, b_down, g1, s1, g2, s2)]
    small = jnp.concatenate(small).T
    first = [w_qkv[t] for t in range(3)] + [small, jnp.zeros((share, 55), bf16)]
    first = jnp.concatenate(first, 1)[None]
    rest = [w_up, w_down.T, w_out.T, jnp.zeros((share, 64), bf16)]
    rest = jnp.concatenate(rest, 1)[None]

    source = me ^ jnp.asarray(np.repeat(gathered_from(stages), share))
    inner = np.tile(np.arange(share), dp)
    outer = np.repeat(np.arange(dp), share)
    place = (outer[:, None] == source[None]) & (inner[:, None] == inner[None])
    place = place.astype(bf16)
    qb = permutation(dp, 6, b_qv.shape[2])
    ub = permutation(dp, 3, b_up.shape[1])

    first = gather_stage(first, stages[0], dp)
    first, rest, x = together(first, rest, prepare(core, inputs))
    rest = gather_stage(rest, stages[0], dp)
    for stage in stages[1:]:
        first = gather_stage(first, stage, dp)
    first, rest, gout = together(first.reshape(D, -1), rest, prepare(core, grad_out))
    first_other = swap(first, "mp", 2, 1)
    for stage in stages[1:]:
        rest = gather_stage(rest, stage, dp)
    n_a = 4
    *done, wq, bq, bu, vec = attend_first(core, x, first, first_other, place, qb, ub, n_a)
    wq, rest = together(wq, rest.reshape(D, -1))
    rest_other = swap(rest, "mp", 2, 1)
    qkv, pts, mixed_t, hat_t = attend_more(core, x, wq, bq, vec, done, n_a)

    output, gres, gmixed, grest, gcol, gbu = feed(
        core, x, gout, mixed_t, rest, rest_other, place, vec, bu
    )

    def reduce_cores(g):
        own = lax.dynamic_index_in_dim(g, core_id, 0, False)
        give = lax.dynamic_index_in_dim(g, 1 - core_id, 0, False)
        total = own.astype(f32) + swap(give, "mp", 2, 1).astype(f32)
        return total.astype(bf16).reshape(dp, share, -1)

    back_stages = stages[::-1]

    def scatter_on(g, index):
        return scatter_stage(g, back_stages[index], dp, index == len(back_stages) - 1)

    grest = reduce_cores(grest)
    output_other = swap(output, "mp", 2, 1)
    first_pairs, pairs = 2, x.shape[0] // G
    state = back(core, gmixed, qkv, pts, hat_t, None, 0, first_pairs)
    dqkv, grest, output_other = together(state[0], grest, output_other)
    state = [dqkv, *state[1:]]
    grest = scatter_on(grest, 0)
    final = (wq, vec, gcol, gbu, qb, ub)
    state = back(core, gmixed, qkv, pts, hat_t, state, first_pairs, pairs - first_pairs, final)
    dqkv, grest, gfirst = together(state[0], grest, state[3])
    for i in range(1, len(back_stages)):
        grest = scatter_on(grest, i)

    gfirst = reduce_cores(gfirst)
    gin = inputs_grad(core, x, gres, dqkv, wq, vec, None, 0, 4)
    gin, gfirst = together(gin, gfirst)
    gfirst = scatter_on(gfirst, 0)
    gin = inputs_grad(core, x, gres, dqkv, wq, vec, gin, 4, 8)
    gin, gfirst = together(gin, gfirst)
    gin_other = swap(gin, "mp", 2, 1)
    for i in range(1, len(back_stages)):
        gfirst = scatter_on(gfirst, i)
    out_full = join(core, output, output_other)
    gin_full = join(core, gin, gin_other)
    gin_full, gfirst, grest = together(gin_full, gfirst, grest)

    gfirst, grest = gfirst[0], grest[0]
    n_q, n_u = w_qkv.shape[2], w_up.shape[1]
    tail = gfirst[:, 3 * n_q : 3 * n_q + 9].T
    gbo, gbd, gg1, gs1, gg2, gs2 = [tail[i] for i in range(3, 9)]
    gw_qkv = jnp.stack([gfirst[:, t * n_q : (t + 1) * n_q] for t in range(3)])
    return (
        out_full,
        gin_full,
        gw_qkv,
        tail[0].reshape(b_qv.shape),
        grest[:, 2 * n_u : 2 * n_u + w_out.shape[0]].T,
        gbo,
        grest[:, :n_u],
        tail[1:3].reshape(b_up.shape),
        grest[:, n_u : 2 * n_u].T,
        gbd,
        gg1,
        gs1,
        gg2,
        gs2,
    )


def solution(mesh):
    specs = (
        P("dp", None),
        P(None, "dp", "mp"),
        P(None, "mp", "dp"),
        P("mp", "dp"),
        P("dp"),
        P("dp", "mp"),
        P("mp", "dp"),
        P("mp", "dp"),
        P("dp"),
        P("dp"),
        P("dp"),
        P("dp"),
        P("dp"),
    )
    dp = mesh.shape["dp"]

    def run(*args):
        return per_device(dp, *args)

    return jax.shard_map(
        run,
        mesh=mesh,
        in_specs=specs + (P("dp", None),),
        out_specs=(P("dp", None),) + specs,
        check_vma=False,
    )
```
